512 devices in a mesh: blk: 32 (over z_lo, x, core), group: 16 (over y, z_hi).
Axes of the slice: x: 4, y: 4, z: 16 (z_hi: 4, z_lo: 4; z = z_hi * 4 + z_lo), core: 2. Of those that a mesh axis runs over, the one named last changes fastest.
Arguments:
- queries: bfloat16 [16, 8192, 4096], P('group', 'blk'), may hold values from -30 to 30
- passages: bfloat16 [16, 512, 4096], P('group', 'blk'), may hold values from -7 to 7
- positives: int32 [16, 8192], P('group', 'blk'), may hold values from 0 to 511
- hard_rows: bfloat16 [16, 512, 4096], P('group', 'blk'), may hold values from -6 to 6
- hard_dest: int32 [16, 512, 1], P('group', 'blk'), may hold values from 0 to 15; in each aligned block of 16 rows (0 to 15, 16 to 31, ..., all dimensions but the last counted through in order) at most 2 rows name the same one
Outputs:
- loss_rows: float32 [16, 8192], P('group', 'blk')
- d_queries: bfloat16 [16, 8192, 4096], P('group', 'blk')
- d_passages: bfloat16 [16, 512, 4096], P('group', 'blk')
- d_hard: bfloat16 [16, 512, 4096], P('group', 'blk')
The draws below stay inside these ranges and needn't reach their ends.
Inputs may be any that keep to these rules, and one draw needn't show every extreme that they name: `hard_dest`: among the 16 hard rows of one device, at most 2 name the same group, and some device reaches 2.
All inputs are finite; a program needn't handle non-finite values.
Results may differ from the reference program's by a relative error of at most 0.0048.
Values may be sent and summed in bfloat16 or wider, within the bound.
No kernel may reach another device: no remote copies, remote signals or barrier semaphores. Data moves between devices by JAX's collectives and lax.ppermute only.
A program may use at most 64 MiB of HBM per device.

```python
import math
import jax
import jax.numpy as jnp
import numpy as np
from jax import lax

EMBED_WIDTH = 4096
Q_DEV = 256
H_DEV = 16
CAP = 2
GROUPS = 16
GROUP_QUERIES = 8192
PROWS = 512
HROWS = 512
N_BLK = 32


def shared_passages(key):
    base = jnp.clip(jax.random.normal(jax.random.fold_in(key, 11), (GROUPS, PROWS, EMBED_WIDTH), jnp.float32), -6.0, 6.0)
    return base


def draw_passages(key, part):
    return shared_passages(key).astype(jnp.bfloat16)


def draw_queries(key, part):
    base = jnp.clip(jax.random.normal(jax.random.fold_in(key, 12), (GROUPS, GROUP_QUERIES, EMBED_WIDTH), jnp.float32), -6.0, 6.0)
    return base.astype(jnp.bfloat16)


def set_ends(values, rng, smallest, high):
    index_at = [jax.random.randint(jax.random.fold_in(rng, axis), (), 0, length) for axis, length in enumerate(values.shape)]
    longest = values.shape.index(max(values.shape))
    beside = index_at[:longest] + [(index_at[longest] + 1) % values.shape[longest]] + index_at[longest + 1:]
    return values.at[tuple(index_at)].set(smallest).at[tuple(beside)].set(high)


def block_scale(key, shape, cuts, smallest, high):
    factor_of, own = 1.0, jax.random.fold_in(key, 6)
    for axis_at, blocks in cuts:
        draws = jnp.exp(jax.random.uniform(jax.random.fold_in(own, axis_at), (blocks,), jnp.float32, smallest / len(cuts), high / len(cuts)))
        factor_of = factor_of * jnp.repeat(draws, shape[axis_at] // blocks).reshape([-1 if axis == axis_at else 1 for axis in range(len(shape))])
    return factor_of


def assign_block(own_key, own, number, rows, count, top, limit, skew):
    sequence = jax.random.permutation(own_key, count)
    heavy_load, ordinary = portions_of(count, rows * top, limit, skew, True), portions_of(count, rows * top, limit, skew, False)
    places = jnp.arange(count)

    def named(tallies, rotation):
        used = int((tallies > 0).sum())
        fixed = max(1, used // 4)
        shifted = fixed + (places - fixed + rotation * (used - fixed)) % max(1, count - fixed)
        return jnp.zeros((count,), jnp.int32).at[sequence[jnp.where(places < fixed, places, shifted)]].set(jnp.asarray(tallies, jnp.int32))

    tallies = jnp.where(number % 4 == 0, named(heavy_load, number // 4), named(ordinary, number - number // 4 - 1))
    mixed = jax.random.permutation(jax.random.fold_in(own, 3), count)
    donor, taker = mixed[0:count // 2 * 2:2], mixed[1:count // 2 * 2:2]
    margin = jnp.minimum(tallies[donor] - 1, limit - tallies[taker]) // 2
    margin = jnp.where((donor == sequence[0]) | (taker == sequence[0]) | (tallies[taker] == 0), 0, jnp.maximum(margin, 0))
    shifted = jax.random.randint(jax.random.fold_in(own, 4), (count // 2,), 0, 1 << 20) % (margin + 1)
    tallies = tallies.at[donor].add(-shifted).at[taker].add(shifted)
    members = jnp.searchsorted(jnp.cumsum(tallies), jnp.arange(rows * top), side="right").astype(jnp.int32)
    table = members.reshape(top, rows).T
    table = table[jax.random.permutation(jax.random.fold_in(own, 1), rows)]
    rotation = jax.random.randint(jax.random.fold_in(own, 2), (rows, 1), 0, top)
    return jnp.take_along_axis(table, (jnp.arange(top)[None, :] + rotation) % top, axis=1)


def portions_of(amount, total, most, lean, full):
    loads = [(1 << 20) // math.isqrt(standing ** lean) + 1 for standing in range(1, amount + 1)]
    largest = most if full else min(most, max(-(-total // amount), total * loads[0] // sum(loads)))
    least = 1 if total - largest >= amount - 1 else 0
    given, rest = [largest] + [least] * (amount - 1), total - largest - least * (amount - 1)
    while rest > 0:
        movable = [i for i in range(1, amount) if given[i] < largest] or [i for i in range(1, amount) if given[i] < most]
        mass, remaining = sum([loads[i] for i in movable]), rest
        for i in movable:
            extra = min(most - given[i], max(1, remaining * loads[i] // mass), rest)
            given[i] = given[i] + extra
            rest = rest - extra
    return np.array(given)


def scatter_about(key, dims, scale, most, shards=(), kind=jnp.bfloat16):
    level = block_scale(key, dims, shards, -0.22, 0.18) if shards else 1.0
    drawn = jax.random.normal(key, dims, jnp.float32) * scale * level
    return jnp.minimum(jnp.maximum(drawn, -most), most).astype(kind)


def setup_inputs(seed: int = 0) -> dict:
    key_list = jax.random.split(jax.random.key(seed), 6)
    queries = draw_queries(jax.random.fold_in(key_list[5], 71), 0)
    passages = draw_passages(jax.random.fold_in(key_list[5], 71), 0)
    positives = set_ends(jax.random.randint(key_list[2], (GROUPS, GROUP_QUERIES), 0, PROWS), jax.random.fold_in(key_list[2], 1), 0, PROWS - 1).astype(jnp.int32)
    hard_rows = scatter_about(key_list[3], (GROUPS, HROWS, EMBED_WIDTH), 1.0, 6.0, ((0, 16), (1, 32)))
    hard_dest_keys = jax.random.split(jax.random.fold_in(key_list[4], 1), GROUPS * HROWS // H_DEV)
    hard_dest_turns = jax.random.permutation(jax.random.fold_in(key_list[4], 3), GROUPS * HROWS // H_DEV)
    hard_dest = jax.vmap(lambda own, number: assign_block(jax.random.fold_in(key_list[4], 2), own, number, H_DEV, GROUPS, 1, CAP, 2))(hard_dest_keys, hard_dest_turns).reshape((GROUPS, HROWS, 1))
    return dict(queries=queries, passages=passages, positives=positives, hard_rows=hard_rows, hard_dest=hard_dest)


def group_terms(query_rows, passage_rows, targets, hard_blocks, route_blocks, group_id):
    score_multiplier = EMBED_WIDTH ** -0.5
    largest_score = lax.Precision.HIGHEST
    in_scores = score_multiplier * jnp.dot(query_rows, passage_rows.T, preferred_element_type=jnp.float32)
    query_tiles = query_rows.reshape(N_BLK, Q_DEV, EMBED_WIDTH).astype(jnp.float32)
    hard_negatives_wide = hard_blocks.astype(jnp.float32)
    is_live = route_blocks == group_id
    negative_scores = score_multiplier * jnp.einsum("pgo,pfo->pgf", query_tiles, hard_negatives_wide, precision=largest_score)
    negative_scores = jnp.where(is_live[:, None, :], negative_scores, -jnp.inf)
    hard_flat = negative_scores.reshape(GROUP_QUERIES, -1)
    run_top = jnp.maximum(jnp.max(in_scores, axis=1), jnp.max(hard_flat, axis=1))
    run_total = jnp.sum(jnp.exp(in_scores - run_top[:, None]), axis=1) + jnp.sum(jnp.exp(hard_flat - run_top[:, None]), axis=1)
    log_total = run_top + jnp.log(run_total)
    prob_in = jnp.exp(in_scores - log_total[:, None])
    hard_probability = jnp.exp(negative_scores - log_total.reshape(N_BLK, Q_DEV)[:, :, None])
    target_hot = (targets[:, None] == jnp.arange(PROWS, dtype=jnp.int32)[None, :]).astype(jnp.float32)
    loss_rows = log_total - jnp.sum(in_scores * target_hot, axis=1)
    coef_in = prob_in - target_hot
    hard_piece = jnp.einsum("sfa,sai->sfi", hard_probability, hard_negatives_wide, precision=largest_score).reshape(GROUP_QUERIES, EMBED_WIDTH)
    d_query = score_multiplier * (jnp.dot(coef_in, passage_rows.astype(jnp.float32), precision=largest_score) + hard_piece)
    coef_round = coef_in.astype(jnp.bfloat16)
    coefficient_blocks = coef_round.reshape(N_BLK, Q_DEV, PROWS).astype(jnp.float32)
    loss_terms = jnp.einsum("luo,luh->loh", coefficient_blocks, query_tiles, precision=largest_score)
    d_passage = (score_multiplier * jnp.sum(loss_terms, axis=0)).astype(jnp.bfloat16)
    hard_exchange_round = lax.optimization_barrier(hard_probability.astype(jnp.bfloat16)).astype(jnp.float32)
    hard_piece_gradient = score_multiplier * jnp.einsum("tmw,tmz->twz", hard_exchange_round, query_tiles, precision=largest_score)
    return loss_rows, d_query.astype(jnp.bfloat16), d_passage, hard_piece_gradient


def reference(queries, passages, positives, hard_rows, hard_dest):
    hard_all = hard_rows.reshape(GROUPS, N_BLK, H_DEV, EMBED_WIDTH).transpose(1, 0, 2, 3).reshape(N_BLK, GROUPS * H_DEV, EMBED_WIDTH)
    route_all = hard_dest[:, :, 0].reshape(GROUPS, N_BLK, H_DEV).transpose(1, 0, 2).reshape(N_BLK, GROUPS * H_DEV)

    def visit(running, inputs):
        query_rows, passage_rows, targets, group_id = inputs
        loss_rows, d_query, d_passage, hard_piece_gradient = group_terms(query_rows, passage_rows, targets, hard_all, route_all, group_id)
        return running + hard_piece_gradient, (loss_rows, d_query, d_passage)

    start_sum = jnp.zeros((N_BLK, GROUPS * H_DEV, EMBED_WIDTH), jnp.float32)
    group_ids = jnp.arange(GROUPS, dtype=jnp.int32)
    hard_sum, outputs = lax.scan(visit, start_sum, (queries, passages, positives, group_ids))
    loss_rows, d_queries, d_passages = outputs
    d_hard = hard_sum.reshape(N_BLK, GROUPS, H_DEV, EMBED_WIDTH).transpose(1, 0, 2, 3).reshape(GROUPS, HROWS, EMBED_WIDTH).astype(jnp.bfloat16)
    return (loss_rows, d_queries, d_passages, d_hard)
```

```python
import jax
import jax.numpy as jnp
from jax import lax
from jax.sharding import PartitionSpec as P

NZ, NX, NC = 4, 4, 2
NY, NH = 4, 4
FLAG = 128
BF16, F32 = jnp.bfloat16, jnp.float32


def blk_perm(dz=0, dx=0, dc=0):
    out = []
    for z in range(NZ):
        for x in range(NX):
            for c in range(NC):
                to = (((z + dz) % NZ) * NX + (x + dx) % NX) * NC + (c + dc) % NC
                out.append(((z * NX + x) * NC + c, to))
    return out


def group_perm(dy=0, dh=0):
    return [
        (y * NH + h, ((y + dy) % NY) * NH + (h + dh) % NH) for y in range(NY) for h in range(NH)
    ]


def dot_t(a, b):
    return lax.dot_general(a, b, (((1,), (1,)), ((), ())), preferred_element_type=F32)


def t_dot(a, b):
    return lax.dot_general(a, b, (((0,), (0,)), ((), ())), preferred_element_type=F32)


def dot(a, b):
    return jnp.dot(a, b, preferred_element_type=F32)


def split(a):
    hi = a.astype(BF16)
    return hi, (a - hi.astype(F32)).astype(BF16)


def body(queries, passages, positives, hard_rows, hard_dest):
    q = queries[0]
    own = passages[0]
    targets = positives[0]
    owned_hard = hard_rows[0]
    routes = hard_dest[0, :, 0]
    width = q.shape[1]
    rows = own.shape[0]
    hard_count = owned_hard.shape[0]
    groups = NY * NH
    slots = max(2, 2 * hard_count // groups)
    scale = width ** (-0.5)
    blk = lax.axis_index("blk")
    grp = lax.axis_index("group")
    my_z, my_x, my_c = blk // (NX * NC), blk // NC % NX, blk % NC
    my_y, my_h = grp // NH, grp % NH

    rel = ((routes // NH - my_y) % NY) * NH + (routes % NH - my_h) % NH
    same = (rel[:, None] == rel[None, :]) & (
        jnp.arange(hard_count)[:, None] > jnp.arange(hard_count)[None, :]
    )
    slot_of = rel * slots + jnp.sum(same.astype(jnp.int32), axis=1)
    placing = (slot_of[None, :] == jnp.arange(groups * slots)[:, None]).astype(BF16)
    wide = jnp.concatenate([owned_hard, jnp.ones((hard_count, FLAG), BF16)], axis=1)
    packed = dot(placing, wide).astype(BF16)
    per_y = NH * slots

    with jax.named_scope("gather_z"):
        parts = [own] + [lax.ppermute(own, "blk", blk_perm(dz=d)) for d in range(1, NZ)]
        z_rows = jnp.concatenate(parts, axis=0)
    with jax.named_scope("hard_y"):
        from_y = [
            packed[d * per_y : (d + 1) * per_y]
            if d == 0
            else lax.ppermute(packed[d * per_y : (d + 1) * per_y], "group", group_perm(dy=d))
            for d in range(NY)
        ]
    with jax.named_scope("gather_x"):
        parts = [z_rows] + [lax.ppermute(z_rows, "blk", blk_perm(dx=d)) for d in range(1, NX)]
        half0 = jnp.concatenate(parts, axis=0)
    with jax.named_scope("hard_h"):
        to_h = [
            jnp.concatenate([f[d * slots : (d + 1) * slots] for f in from_y], axis=0)
            for d in range(NH)
        ]
        received = jnp.concatenate(
            [
                to_h[d] if d == 0 else lax.ppermute(to_h[d], "group", group_perm(dh=d))
                for d in range(NH)
            ],
            axis=0,
        )
    with jax.named_scope("gather_core"):
        half1 = lax.ppermute(half0, "blk", blk_perm(dc=1))

    hard = received[:, :width]
    live = received[:, width] > 0.5
    half = half0.shape[0]

    owner = targets // rows
    o_z, o_x, o_c = owner // (NX * NC), owner // NC % NX, owner % NC
    column = (
        ((my_c - o_c) % NC) * half
        + (((my_x - o_x) % NX) * NZ + (my_z - o_z) % NZ) * rows
        + targets % rows
    )
    hot0 = column[:, None] == jnp.arange(half)[None, :]
    hot1 = column[:, None] == (jnp.arange(half) + half)[None, :]

    with jax.named_scope("scores"):
        s0 = scale * dot_t(q, half0)
        s1 = scale * dot_t(q, half1)
        sh = jnp.where(live[None, :], scale * dot_t(q, hard), -jnp.inf)
        top = jnp.maximum(
            jnp.maximum(jnp.max(s0, axis=1), jnp.max(s1, axis=1)), jnp.max(sh, axis=1)
        )
        total = (
            jnp.sum(jnp.exp(s0 - top[:, None]), axis=1)
            + jnp.sum(jnp.exp(s1 - top[:, None]), axis=1)
            + jnp.sum(jnp.exp(sh - top[:, None]), axis=1)
        )
        log_total = top + jnp.log(total)
        c0 = jnp.exp(s0 - log_total[:, None]) - hot0.astype(F32)
        c1 = jnp.exp(s1 - log_total[:, None]) - hot1.astype(F32)
        ph = jnp.exp(sh - log_total[:, None])
        at_target = jnp.sum(jnp.where(hot0, s0, 0.0), axis=1) + jnp.sum(
            jnp.where(hot1, s1, 0.0), axis=1
        )
        loss_rows = log_total - at_target

    c0_hi, c0_lo = split(c0)
    c1_hi, c1_lo = split(c1)
    ph_hi, ph_lo = split(ph)
    with jax.named_scope("scatter_core"):
        away = t_dot(c1_hi, q).astype(BF16)
        away = lax.ppermute(away, "blk", blk_perm(dc=1))
    with jax.named_scope("hard_grad"):
        g = (scale * t_dot(ph_hi, q)).astype(BF16)
    with jax.named_scope("scatter_x"):
        total0 = t_dot(c0_hi, q) + away.astype(F32)
        n = half // NX
        acc = total0[:n]
        for d in range(1, NX):
            acc = acc + lax.ppermute(
                total0[d * n : (d + 1) * n].astype(BF16), "blk", blk_perm(dx=-d)
            ).astype(F32)
    with jax.named_scope("hard_grad_h"):
        per_h = NY * slots
        back_h = [
            g[d * per_h : (d + 1) * per_h]
            if d == 0
            else lax.ppermute(g[d * per_h : (d + 1) * per_h], "group", group_perm(dh=-d))
            for d in range(NH)
        ]
    with jax.named_scope("scatter_z"):
        fin = acc[:rows]
        for d in range(1, NZ):
            fin = fin + lax.ppermute(
                acc[d * rows : (d + 1) * rows].astype(BF16), "blk", blk_perm(dz=-d)
            ).astype(F32)
        d_passage = (scale * fin).astype(BF16)
    with jax.named_scope("hard_grad_y"):
        to_y = [
            jnp.concatenate([b[d * slots : (d + 1) * slots] for b in back_h], axis=0)
            for d in range(NY)
        ]
        returned = jnp.concatenate(
            [
                to_y[d] if d == 0 else lax.ppermute(to_y[d], "group", group_perm(dy=-d))
                for d in range(NY)
            ],
            axis=0,
        )
        d_owned = t_dot(placing, returned).astype(BF16)

    with jax.named_scope("d_query"):
        d_query = scale * (
            (dot(c0_hi, half0) + dot(c1_hi, half1) + dot(ph_hi, hard))
            + (dot(c0_lo, half0) + dot(c1_lo, half1) + dot(ph_lo, hard))
        )
    return (loss_rows[None], d_query.astype(BF16)[None], d_passage[None], d_owned[None])


def solution(mesh):
    return jax.shard_map(
        body,
        mesh=mesh,
        in_specs=(
            P("group", "blk", None),
            P("group", "blk", None),
            P("group", "blk"),
            P("group", "blk", None),
            P("group", "blk", None),
        ),
        out_specs=(
            P("group", "blk"),
            P("group", "blk", None),
            P("group", "blk", None),
            P("group", "blk", None),
        ),
        check_vma=False,
    )
```

```python
import jax
import jax.numpy as jnp
import numpy as np
from jax import lax
from jax.sharding import PartitionSpec as P

NZ, NX, NC = 4, 4, 2
NY, NH = 4, 4
Y_GROUPS = [[y * NH + h for y in range(NY)] for h in range(NH)]
H_GROUPS = [[y * NH + h for h in range(NH)] for y in range(NY)]
FLAG = 128
BF16, F32 = jnp.bfloat16, jnp.float32


def blk_perm(dz=0, dx=0, dc=0):
    out = []
    for z in range(NZ):
        for x in range(NX):
            for c in range(NC):
                to = (((z + dz) % NZ) * NX + (x + dx) % NX) * NC + (c + dc) % NC
                out.append(((z * NX + x) * NC + c, to))
    return out


def dot_t(a, b):
    return lax.dot_general(a, b, (((1,), (1,)), ((), ())), preferred_element_type=F32)


def t_dot(a, b):
    return lax.dot_general(a, b, (((0,), (0,)), ((), ())), preferred_element_type=F32)


def dot(a, b):
    return jnp.dot(a, b, preferred_element_type=F32)


def split(a):
    hi = a.astype(BF16)
    return hi, (a - hi.astype(F32)).astype(BF16)


def body(queries, passages, positives, hard_rows, hard_dest):
    q = queries[0]
    own = passages[0]
    targets = positives[0]
    owned_hard = hard_rows[0]
    routes = hard_dest[0, :, 0]
    width = q.shape[1]
    rows = own.shape[0]
    hard_count = owned_hard.shape[0]
    groups = lax.axis_size("group")
    slots = max(2, 2 * hard_count // groups)
    scale = width ** (-0.5)
    blk = lax.axis_index("blk")
    my_z, my_x, my_c = blk // (NX * NC), blk // NC % NX, blk % NC

    same = (routes[:, None] == routes[None, :]) & (
        jnp.arange(hard_count)[:, None] > jnp.arange(hard_count)[None, :]
    )
    slot_of = routes * slots + jnp.sum(same.astype(jnp.int32), axis=1)
    placing = (slot_of[None, :] == jnp.arange(groups * slots)[:, None]).astype(BF16)
    wide = jnp.concatenate([owned_hard, jnp.ones((hard_count, FLAG), BF16)], axis=1)
    packed = dot(placing, wide).astype(BF16)

    with jax.named_scope("gather_z"):
        parts = [own] + [lax.ppermute(own, "blk", blk_perm(dz=d)) for d in range(1, NZ)]
        z_rows = jnp.concatenate(parts, axis=0)
    with jax.named_scope("hard_y"):
        from_y = lax.all_to_all(
            packed, "group", split_axis=0, concat_axis=0, axis_index_groups=Y_GROUPS, tiled=True
        )
        order = np.arange(groups * slots).reshape(NY, NH, slots).transpose(1, 0, 2).reshape(-1)
        turn = jnp.asarray(order[:, None] == np.arange(groups * slots)[None, :], BF16)
        to_h = dot(turn, from_y).astype(BF16)
        z_rows, to_h = lax.optimization_barrier((z_rows, to_h))
    with jax.named_scope("hard_h"):
        received = lax.all_to_all(
            to_h, "group", split_axis=0, concat_axis=0, axis_index_groups=H_GROUPS, tiled=True
        )
    with jax.named_scope("gather_x"):
        parts = [z_rows] + [lax.ppermute(z_rows, "blk", blk_perm(dx=d)) for d in range(1, NX)]
        *parts, received = lax.optimization_barrier((*parts, received))
        half0 = jnp.concatenate(parts, axis=0)
    with jax.named_scope("gather_core"):
        half1 = lax.ppermute(half0, "blk", blk_perm(dc=1))

    hard = received[:, :width]
    live = received[:, width] > 0.5
    half = half0.shape[0]

    owner = targets // rows
    o_z, o_x, o_c = owner // (NX * NC), owner // NC % NX, owner % NC
    column = (
        ((my_c - o_c) % NC) * half
        + (((my_x - o_x) % NX) * NZ + (my_z - o_z) % NZ) * rows
        + targets % rows
    )
    hot0 = column[:, None] == jnp.arange(half)[None, :]
    hot1 = column[:, None] == (jnp.arange(half) + half)[None, :]

    with jax.named_scope("scores"):
        s0 = scale * dot_t(q, half0)
        s1 = scale * dot_t(q, half1)
        sh = jnp.where(live[None, :], scale * dot_t(q, hard), -jnp.inf)
        top = jnp.maximum(
            jnp.maximum(jnp.max(s0, axis=1), jnp.max(s1, axis=1)), jnp.max(sh, axis=1)
        )
        total = (
            jnp.sum(jnp.exp(s0 - top[:, None]), axis=1)
            + jnp.sum(jnp.exp(s1 - top[:, None]), axis=1)
            + jnp.sum(jnp.exp(sh - top[:, None]), axis=1)
        )
        log_total = top + jnp.log(total)
        c0 = jnp.exp(s0 - log_total[:, None]) - hot0.astype(F32)
        c1 = jnp.exp(s1 - log_total[:, None]) - hot1.astype(F32)
        ph = jnp.exp(sh - log_total[:, None])
        at_target = jnp.sum(jnp.where(hot0, s0, 0.0), axis=1) + jnp.sum(
            jnp.where(hot1, s1, 0.0), axis=1
        )
        loss_rows = log_total - at_target

    c0_hi, c0_lo = split(c0)
    c1_hi, c1_lo = split(c1)
    ph_hi, ph_lo = split(ph)
    with jax.named_scope("scatter_core"):
        away = t_dot(c1_hi, q).astype(BF16)
        away = lax.ppermute(away, "blk", blk_perm(dc=1))
    with jax.named_scope("hard_grad"):
        ph_late, _ = lax.optimization_barrier((ph_hi, away))
        g = (scale * t_dot(dot(ph_late, turn).astype(BF16), q)).astype(BF16)
    with jax.named_scope("scatter_x"):
        total0 = t_dot(c0_hi, q) + away.astype(F32)
        n = half // NX
        acc = total0[:n]
        for d in range(1, NX):
            acc = acc + lax.ppermute(
                total0[d * n : (d + 1) * n].astype(BF16), "blk", blk_perm(dx=-d)
            ).astype(F32)
    with jax.named_scope("hard_back"):
        returned = lax.all_to_all(
            g.reshape(groups, slots, width), "group", split_axis=0, concat_axis=0, tiled=True
        ).reshape(groups * slots, width)
    c0_hi, c0_lo, c1_hi, c1_lo, ph_hi, ph_lo, _ = lax.optimization_barrier(
        (c0_hi, c0_lo, c1_hi, c1_lo, ph_hi, ph_lo, away)
    )
    with jax.named_scope("scatter_z"):
        fin = acc[:rows]
        for d in range(1, NZ):
            fin = fin + lax.ppermute(
                acc[d * rows : (d + 1) * rows].astype(BF16), "blk", blk_perm(dz=-d)
            ).astype(F32)
        d_passage = (scale * fin).astype(BF16)
    with jax.named_scope("hard_own"):
        d_owned = t_dot(placing, returned).astype(BF16)

    with jax.named_scope("d_query"):
        d_query = scale * (
            (dot(c0_hi, half0) + dot(c1_hi, half1) + dot(ph_hi, hard))
            + (dot(c0_lo, half0) + dot(c1_lo, half1) + dot(ph_lo, hard))
        )
    return (loss_rows[None], d_query.astype(BF16)[None], d_passage[None], d_owned[None])


def solution(mesh):
    return jax.shard_map(
        body,
        mesh=mesh,
        in_specs=(
            P("group", "blk", None),
            P("group", "blk", None),
            P("group", "blk"),
            P("group", "blk", None),
            P("group", "blk", None),
        ),
        out_specs=(
            P("group", "blk"),
            P("group", "blk", None),
            P("group", "blk", None),
            P("group", "blk", None),
        ),
        check_vma=False,
    )
```

```python
import functools

import jax
import jax.numpy as jnp
from jax import lax
from jax.experimental import pallas as pl
from jax.experimental.pallas import tpu as pltpu
from jax.sharding import PartitionSpec as P

NZ, NX, NC = 4, 4, 2
NY, NH = 4, 4
X_GROUPS = [
    [(z * NX + x) * NC + c for x in range(NX)] for z in range(NZ) for c in range(NC)
]
Y_GROUPS = [[y * NH + h for y in range(NY)] for h in range(NH)]
CORE_SWAP = [(i, i ^ 1) for i in range(NZ * NX * NC)]
FLAG = 128
BF16, F32 = jnp.bfloat16, jnp.float32


def z_shift(d):
    step = NX * NC
    return [(i, (i // step + d) % NZ * step + i % step) for i in range(NZ * step)]


def x_shift(d):
    step = NX * NC
    return [(i, i // step * step + (i + d * NC) % step) for i in range(NZ * step)]


def h_shift(d):
    return [(i, i // NH * NH + (i + d) % NH) for i in range(NY * NH)]


def exchange(parts, axis, perm, sign=1):
    return parts[:1] + [lax.ppermute(p, axis, perm(sign * d)) for d, p in enumerate(parts) if d]


def pieces(x, n):
    k = x.shape[0] // n
    return [x[i * k : (i + 1) * k] for i in range(n)]


def turn(parts, n):
    cut = [pieces(p, n) for p in parts]
    return [jnp.concatenate([c[i] for c in cut], axis=0) for i in range(n)]


def dot_t(a, b):
    return lax.dot_general(a, b, (((1,), (1,)), ((), ())), preferred_element_type=F32)


def t_dot(a, b):
    return lax.dot_general(a, b, (((0,), (0,)), ((), ())), preferred_element_type=F32)


def dot(a, b):
    return jnp.dot(a, b, preferred_element_type=F32)


def split(a):
    hi = a.astype(BF16)
    return hi, (a - hi.astype(F32)).astype(BF16)


def swap(x, axis, members):
    return lax.all_to_all(
        x, axis, split_axis=0, concat_axis=0, axis_index_groups=members, tiled=True
    )


def pack_kernel(slots, h_ref, dest_ref, rows_ref, packed_ref, placing_ref):
    dest = dest_ref[...]
    count, width = rows_ref.shape
    groups = NY * NH
    hot = (dest == lax.broadcasted_iota(jnp.int32, (count, groups), 1)).astype(F32)
    ahead = (
        lax.broadcasted_iota(jnp.int32, (count, count), 0)
        > lax.broadcasted_iota(jnp.int32, (count, count), 1)
    ).astype(F32)
    rank = jnp.sum(dot(ahead, hot) * hot, axis=1, keepdims=True).astype(jnp.int32)
    at = lax.broadcasted_iota(jnp.int32, (count, groups * slots), 1)
    h = dest % NH
    step = h - h_ref[0]
    step = jnp.where(step < 0, step + NH, step)
    send = ((dest - h + step) * slots + rank == at).astype(BF16)
    packed_ref[:, :width] = t_dot(send, rows_ref[...]).astype(BF16)
    packed_ref[:, width:] = t_dot(send, jnp.ones((count, FLAG), BF16)).astype(BF16)
    placing_ref[...] = (dest * slots + rank == at).astype(BF16)


def pack(dest, rows, my_h, slots):
    count, width = rows.shape
    places = NY * NH * slots
    return pl.pallas_call(
        functools.partial(pack_kernel, slots),
        in_specs=[
            pl.BlockSpec(memory_space=pltpu.SMEM),
            pl.BlockSpec(memory_space=pltpu.VMEM),
            pl.BlockSpec(memory_space=pltpu.VMEM),
        ],
        out_specs=[pl.BlockSpec(memory_space=pltpu.VMEM)] * 2,
        out_shape=[
            jax.ShapeDtypeStruct((places, width + FLAG), BF16),
            jax.ShapeDtypeStruct((count, places), BF16),
        ],
        cost_estimate=pl.CostEstimate(
            flops=2 * count * places * width, bytes_accessed=6 * places * width, transcendentals=0
        ),
        name="pack",
    )(my_h.reshape(1), dest, rows)


def core_sum_kernel(coef_ref, q_ref, away_ref, own_ref, *sent_refs):
    total = t_dot(coef_ref[...], q_ref[...]) + away_ref[...].astype(F32)
    n = own_ref.shape[0]
    own_ref[...] = total[:n]
    for d, ref in enumerate(sent_refs):
        ref[...] = total[(d + 1) * n : (d + 2) * n].astype(BF16)


def core_sum(coef, q, away, block=512):
    count, width = q.shape
    half = coef.shape[1]
    n = half // NX
    return pl.pallas_call(
        core_sum_kernel,
        grid=(width // block,),
        in_specs=[
            pl.BlockSpec((count, half), lambda i: (0, 0)),
            pl.BlockSpec((count, block), lambda i: (0, i)),
            pl.BlockSpec((half, block), lambda i: (0, i)),
        ],
        out_specs=[pl.BlockSpec((n, block), lambda i: (0, i))] * NX,
        out_shape=[jax.ShapeDtypeStruct((n, width), F32)]
        + [jax.ShapeDtypeStruct((n, width), BF16)] * (NX - 1),
        cost_estimate=pl.CostEstimate(
            flops=2 * count * half * width, bytes_accessed=6 * half * width, transcendentals=0
        ),
        compiler_params=pltpu.CompilerParams(vmem_limit_bytes=16 << 20),
        name="core_sum",
    )(coef, q, away)


def query_grad_kernel(scale, *refs):
    coefs, rows, out = refs[:6], refs[6:9], refs[9]
    total = dot(coefs[0][...], rows[0][...])
    for i in range(1, 6):
        total = total + dot(coefs[i][...], rows[i % 3][...])
    out[0] = (scale * total).astype(out.dtype)


def query_grad(coefs, rows, scale, block=512):
    count, width = coefs[0].shape[0], rows[0].shape[1]
    return pl.pallas_call(
        functools.partial(query_grad_kernel, scale),
        grid=(width // block,),
        in_specs=[pl.BlockSpec(c.shape, lambda i: (0, 0)) for c in coefs]
        + [pl.BlockSpec((r.shape[0], block), lambda i: (0, i)) for r in rows],
        out_specs=pl.BlockSpec((1, count, block), lambda i: (0, 0, i)),
        out_shape=jax.ShapeDtypeStruct((1, count, width), BF16),
        cost_estimate=pl.CostEstimate(
            flops=4 * count * width * sum(r.shape[0] for r in rows),
            bytes_accessed=2 * width * (count + sum(r.shape[0] for r in rows)),
            transcendentals=0,
        ),
        compiler_params=pltpu.CompilerParams(vmem_limit_bytes=16 << 20),
        name="query_grad",
    )(*coefs, *rows)


def body(queries, passages, positives, hard_rows, hard_dest):
    q = queries[0]
    own = passages[0]
    targets = positives[0]
    owned_hard = hard_rows[0]
    width = q.shape[1]
    rows = own.shape[0]
    groups = NY * NH
    slots = max(2, 2 * owned_hard.shape[0] // groups)
    scale = width ** (-0.5)
    blk = lax.axis_index("blk")
    my_z, my_x, my_c = blk // (NX * NC), blk // NC % NX, blk % NC
    my_h = lax.axis_index("group") % NH

    packed, placing = pack(hard_dest[0], owned_hard, my_h, slots)
    own, packed = lax.optimization_barrier((own, packed))

    with jax.named_scope("gather_z"):
        z_rows = jnp.concatenate(exchange([own] * NZ, "blk", z_shift), axis=0)
    with jax.named_scope("hard_y"):
        from_y = pieces(swap(packed, "group", Y_GROUPS), NY)
    with jax.named_scope("gather_x"):
        z_rows = lax.optimization_barrier(z_rows)
        spread = jnp.broadcast_to(z_rows, (NX, *z_rows.shape)).reshape(-1, width)
        half0 = swap(spread, "blk", X_GROUPS)
    with jax.named_scope("hard_h"):
        received = jnp.concatenate(exchange(turn(from_y, NH), "group", h_shift), axis=0)
    half0, received = lax.optimization_barrier((half0, received))
    with jax.named_scope("gather_core"):
        half1 = lax.ppermute(half0, "blk", CORE_SWAP)

    hard = received[:, :width]
    live = received[:, width] > 0.5
    half = half0.shape[0]

    owner = targets // rows
    o_z, o_x, o_c = owner // (NX * NC), owner // NC % NX, owner % NC
    column = (o_c != my_c).astype(jnp.int32) * half + (o_x * NZ + (my_z - o_z) % NZ) * rows + targets % rows
    hot0 = column[:, None] == jnp.arange(half)[None, :]
    hot1 = column[:, None] == (jnp.arange(half) + half)[None, :]

    with jax.named_scope("scores"):
        s0 = scale * dot_t(q, half0)
        s1 = scale * dot_t(q, half1)
        sh = jnp.where(live[None, :], scale * dot_t(q, hard), -jnp.inf)
        top = jnp.maximum(
            jnp.maximum(jnp.max(s0, axis=1), jnp.max(s1, axis=1)), jnp.max(sh, axis=1)
        )
        total = (
            jnp.sum(jnp.exp(s0 - top[:, None]), axis=1)
            + jnp.sum(jnp.exp(s1 - top[:, None]), axis=1)
            + jnp.sum(jnp.exp(sh - top[:, None]), axis=1)
        )
        log_total = top + jnp.log(total)
        c0 = jnp.exp(s0 - log_total[:, None]) - hot0.astype(F32)
        c1 = jnp.exp(s1 - log_total[:, None]) - hot1.astype(F32)
        ph = jnp.exp(sh - log_total[:, None])
        at_target = jnp.sum(jnp.where(hot0, s0, 0.0), axis=1) + jnp.sum(
            jnp.where(hot1, s1, 0.0), axis=1
        )
        loss_rows = log_total - at_target

    c0_hi, c0_lo = split(c0)
    c1_hi, c1_lo = split(c1)
    ph_hi, ph_lo = split(ph)
    n = half // NX
    col = jnp.arange(half)
    back_x = (my_x - col // n) % NX * n + col % n
    roll = (col[:, None] == back_x[None, :]).astype(BF16)
    with jax.named_scope("scatter_core"):
        away = t_dot(dot(c1_hi, roll).astype(BF16), q).astype(BF16)
        away = lax.ppermute(away, "blk", CORE_SWAP)
    with jax.named_scope("scatter_x"):
        mine = core_sum(dot(c0_hi, roll).astype(BF16), q, away)
        chunks = [c.astype(F32) for c in exchange(list(mine), "blk", x_shift, -1)]
        mine_x = pieces(functools.reduce(jnp.add, chunks), NZ)

    c0_hi, c0_lo, c1_hi, c1_lo, ph_hi, ph_lo, _ = lax.optimization_barrier(
        (c0_hi, c0_lo, c1_hi, c1_lo, ph_hi, ph_lo, away)
    )
    with jax.named_scope("hard_back"):
        at = jnp.arange(groups * slots)
        step, y, slot = at // (NY * slots), at // slots % NY, at % slots
        to = (y * NH + (my_h - step) % NH) * slots + slot
        order = (to[:, None] == at[None, :]).astype(BF16)
        g = (scale * t_dot(dot(ph_hi, order).astype(BF16), q)).astype(BF16)
        returned = lax.all_to_all(
            g.reshape(groups, slots, width), "group", split_axis=0, concat_axis=0, tiled=True
        ).reshape(groups * slots, width)
    with jax.named_scope("scatter_z"):
        sent = [mine_x[0]] + [m.astype(BF16) for m in mine_x[1:]]
        chunks = [c.astype(F32) for c in exchange(sent, "blk", z_shift, -1)]
        d_passage = (scale * functools.reduce(jnp.add, chunks)).astype(BF16)
    with jax.named_scope("hard_own"):
        d_owned = dot(placing, returned).astype(BF16)
    with jax.named_scope("d_query"):
        d_query = query_grad(
            (c0_hi, c1_hi, ph_hi, c0_lo, c1_lo, ph_lo), (half0, half1, hard), scale
        )
    return (loss_rows[None], d_query, d_passage[None], d_owned[None])


def solution(mesh):
    return jax.shard_map(
        body,
        mesh=mesh,
        in_specs=(
            P("group", "blk", None),
            P("group", "blk", None),
            P("group", "blk"),
            P("group", "blk", None),
            P("group", "blk", None),
        ),
        out_specs=(
            P("group", "blk"),
            P("group", "blk", None),
            P("group", "blk", None),
            P("group", "blk", None),
        ),
        check_vma=False,
    )
```

```python
import functools

import jax
import jax.numpy as jnp
from jax import lax
from jax.experimental import pallas as pl
from jax.experimental.pallas import tpu as pltpu
from jax.sharding import PartitionSpec as P

NZ, NX, NC = 4, 4, 2
CORE_SWAP = [(i, i ^ 1) for i in range(NZ * NX * NC)]
FLAG = 128
BF16, F32 = jnp.bfloat16, jnp.float32


def z_shift(d):
    step = NX * NC
    return [(i, (i // step + d) % NZ * step + i % step) for i in range(NZ * step)]


def x_shift(d):
    step = NX * NC
    return [(i, i // step * step + (i + d * NC) % step) for i in range(NZ * step)]


def exchange(parts, axis, perm, sign=1):
    return parts[:1] + [lax.ppermute(p, axis, perm(sign * d)) for d, p in enumerate(parts) if d]


def pieces(x, n):
    k = x.shape[0] // n
    return [x[i * k : (i + 1) * k] for i in range(n)]


def dot_t(a, b):
    return lax.dot_general(a, b, (((1,), (1,)), ((), ())), preferred_element_type=F32)


def t_dot(a, b):
    return lax.dot_general(a, b, (((0,), (0,)), ((), ())), preferred_element_type=F32)


def dot(a, b):
    return jnp.dot(a, b, preferred_element_type=F32)


def split(a):
    hi = a.astype(BF16)
    return hi, (a - hi.astype(F32)).astype(BF16)


def iota(dims, dim):
    return lax.broadcasted_iota(jnp.int32, dims, dim)


def shape(dims, dtype=BF16):
    return jax.ShapeDtypeStruct(dims, dtype)


def call(kernel, outs, args, name, flops, grant, scalars=1):
    size = sum(a.size * a.dtype.itemsize for a in (*args, *outs))
    return pl.pallas_call(
        kernel,
        in_specs=[pl.BlockSpec(memory_space=pltpu.SMEM)] * scalars
        + [pl.BlockSpec(memory_space=pltpu.VMEM)] * (len(args) - scalars),
        out_specs=[pl.BlockSpec(memory_space=pltpu.VMEM)] * len(outs),
        out_shape=outs,
        cost_estimate=pl.CostEstimate(flops=flops, bytes_accessed=size, transcendentals=0),
        compiler_params=pltpu.CompilerParams(vmem_limit_bytes=grant << 20),
        name=name,
    )(*args)


def over_columns(width, step, block=512):
    @pl.loop(0, width // block)
    def _(i):
        step(pl.ds(pl.multiple_of(i * block, block), block))


def joined(refs, cols=slice(None)):
    return jnp.concatenate([r[:, cols] for r in refs], axis=0)


def flip(x):
    n = x.shape[1]
    return dot_t((iota((n, n), 0) == iota((n, n), 1)).astype(BF16), x).astype(BF16)


def pack_kernel(groups, slots, dest_ref, rows_ref, packed_ref, placing_ref):
    dest = dest_ref[...]
    count, width = rows_ref.shape
    hot = (dest == iota((groups, count), 0)).astype(F32)
    ahead = (iota((count, count), 0) < iota((count, count), 1)).astype(F32)
    rank = jnp.sum(dot(hot, ahead) * hot, axis=0, keepdims=True).astype(jnp.int32)
    placing = (dest * slots + rank == iota((groups * slots, count), 0)).astype(BF16)
    packed_ref[:, :width] = dot(placing, rows_ref[...]).astype(BF16)
    packed_ref[:, width:] = dot(placing, jnp.ones((count, FLAG), BF16)).astype(BF16)
    placing_ref[...] = placing


def near_kernel(scale, q_ref, *refs):
    refs[-1][...] = scale * dot_t(q_ref[...], joined(refs[:-1]))


def coef_kernel(
    scale, q_ref, far0, far1, far2, far3, got_ref, s0_ref, column_ref,
    away_ref, mine_ref, hard_ref, hi0_ref, lo0_ref, hi1_ref, lo1_ref, hih_ref, loh_ref, loss_ref,
):
    count, width = q_ref.shape
    q, s0 = q_ref[...], s0_ref[...]
    half = s0.shape[1]
    s1 = scale * dot_t(q, joined((far0, far1, far2, far3)))
    flags = dot_t(jnp.ones((count, FLAG), BF16), got_ref[:, width:])
    sh = jnp.where(flags > 0.5 * FLAG, scale * dot_t(q, got_ref[:, :width]), -jnp.inf)
    top = jnp.maximum(
        jnp.max(jnp.maximum(s0, s1), axis=1, keepdims=True), jnp.max(sh, axis=1, keepdims=True)
    )
    total = jnp.sum(jnp.exp(s0 - top) + jnp.exp(s1 - top), axis=1, keepdims=True)
    total = total + jnp.sum(jnp.exp(sh - top), axis=1, keepdims=True)
    log_total = top + jnp.log(total)
    column = column_ref[...]
    hot0 = column == iota((count, half), 1)
    hot1 = column == iota((count, half), 1) + half
    at_target = jnp.sum(jnp.where(hot0, s0, 0.0) + jnp.where(hot1, s1, 0.0), axis=1, keepdims=True)
    loss_ref[...] = log_total - at_target
    hi1, lo1 = split(jnp.exp(s1 - log_total) - hot1.astype(F32))
    away = flip(hi1)

    def send(cols):
        away_ref[:, cols] = dot(away, q_ref[:, cols]).astype(BF16)

    over_columns(width, send)
    hi1_ref[...], lo1_ref[...] = hi1, lo1
    hi0, lo0 = split(jnp.exp(s0 - log_total) - hot0.astype(F32))
    hi0_ref[...], lo0_ref[...] = hi0, lo0
    mine_ref[...] = flip(hi0)
    hih, loh = split(jnp.exp(sh - log_total))
    hih_ref[...], loh_ref[...] = hih, loh
    hard_ref[...] = flip(hih)


def core_sum_kernel(coef_ref, q_ref, away_ref, own_ref, *sent_refs):
    n = own_ref.shape[0]

    def add(cols):
        total = dot(coef_ref[...], q_ref[:, cols]) + away_ref[:, cols].astype(F32)
        own_ref[:, cols] = total[:n]
        for d, ref in enumerate(sent_refs):
            ref[:, cols] = total[(d + 1) * n : (d + 2) * n].astype(BF16)

    over_columns(q_ref.shape[1], add)


def query_grad_kernel(scale, *refs):
    coefs, near, far, got, out = refs[:6], refs[6:10], refs[10:14], refs[14], refs[15]

    def grad(cols):
        rows = (joined(near, cols), joined(far, cols), got[:, cols])
        total = dot(coefs[0][...], rows[0])
        for i in range(1, 6):
            total = total + dot(coefs[i][...], rows[i % 3])
        out[0, :, cols] = (scale * total).astype(out.dtype)

    over_columns(out.shape[2], grad)


def body(queries, passages, positives, hard_rows, hard_dest):
    q = queries[0]
    own = passages[0]
    targets = positives[0]
    owned_hard = hard_rows[0]
    count, width = q.shape
    rows = own.shape[0]
    groups = lax.axis_size("group")
    slots = max(2, 2 * owned_hard.shape[0] // groups)
    half, places = NZ * NX * rows, groups * slots
    scale = width ** (-0.5)
    blk = lax.axis_index("blk")
    my_z, my_x, my_c = blk // (NX * NC), blk // NC % NX, blk % NC

    with jax.named_scope("gather_z"):
        z_rows = jnp.concatenate(exchange([own] * NZ, "blk", z_shift), axis=0)
    with jax.named_scope("hard_out"):
        packed, placing = call(
            functools.partial(pack_kernel, groups, slots),
            [shape((places, width + FLAG)), shape((places, owned_hard.shape[0]))],
            (hard_dest.reshape(1, -1), owned_hard),
            "pack", 2 * places * owned_hard.size, 2, 0,
        )
        received = lax.all_to_all(
            packed.reshape(groups, slots, -1), "group", split_axis=0, concat_axis=0, tiled=True
        ).reshape(places, -1)
    with jax.named_scope("gather_x"):
        near = exchange([z_rows] * NX, "blk", x_shift)
        near[-1], received = lax.optimization_barrier((near[-1], received))
    with jax.named_scope("gather_core"):
        far = [lax.ppermute(x, "blk", CORE_SWAP) for x in near]

    owner = targets // rows
    o_z, o_x, o_c = owner // (NX * NC), owner // NC % NX, owner % NC
    column = (
        (o_c != my_c).astype(jnp.int32) * half
        + ((my_x - o_x) % NX * NZ + (my_z - o_z) % NZ) * rows
        + targets % rows
    )
    with jax.named_scope("scores"):
        [s0] = call(
            functools.partial(near_kernel, scale),
            [shape((count, half), F32)],
            (q, *near),
            "near", 2 * count * half * width, 8, 0,
        )
        square, thin = shape((count, half)), shape((count, places))
        away, mine_rows, hard_cols, hi0, lo0, hi1, lo1, hih, loh, loss_rows = call(
            functools.partial(coef_kernel, scale),
            [
                shape((half, width)), shape((half, count)), shape((places, count)),
                square, square, square, square, thin, thin, shape((count, 1), F32),
            ],
            (q, *far, received, s0, column.reshape(-1, 1)),
            "coef", 4 * count * half * width, 12, 0,
        )
    with jax.named_scope("scatter_core"):
        away = lax.ppermute(away, "blk", CORE_SWAP)
    with jax.named_scope("scatter_x"):
        n = half // NX
        mine = call(
            core_sum_kernel,
            [shape((n, width), F32)] + [shape((n, width))] * (NX - 1),
            (mine_rows, q, away),
            "core_sum", 2 * count * half * width, 8, 0,
        )
        chunks = [c.astype(F32) for c in exchange(list(mine), "blk", x_shift, -1)]
        mine_x = pieces(functools.reduce(jnp.add, chunks), NZ)

    hard_cols, hi0, _ = lax.optimization_barrier((hard_cols, hi0, away))
    with jax.named_scope("hard_back"):
        g = (scale * dot(hard_cols, q)).astype(BF16)
        returned = lax.all_to_all(
            g.reshape(groups, slots, width), "group", split_axis=0, concat_axis=0, tiled=True
        ).reshape(places, width)
        d_owned = t_dot(placing, returned).astype(BF16)
    with jax.named_scope("d_query"):
        [d_query] = call(
            functools.partial(query_grad_kernel, scale),
            [shape((1, count, width))],
            (hi0, hi1, hih, lo0, lo1, loh, *near, *far, received),
            "query_grad", 4 * count * (2 * half + places) * width, 8, 0,
        )
    with jax.named_scope("scatter_z"):
        sent = [mine_x[0]] + [m.astype(BF16) for m in mine_x[1:]]
        chunks = [c.astype(F32) for c in exchange(sent, "blk", z_shift, -1)]
        d_passage = (scale * functools.reduce(jnp.add, chunks)).astype(BF16)
    return (loss_rows.reshape(1, -1), d_query, d_passage[None], d_owned[None])


def solution(mesh):
    return jax.shard_map(
        body,
        mesh=mesh,
        in_specs=(
            P("group", "blk", None),
            P("group", "blk", None),
            P("group", "blk"),
            P("group", "blk", None),
            P("group", "blk", None),
        ),
        out_specs=(
            P("group", "blk"),
            P("group", "blk", None),
            P("group", "blk", None),
            P("group", "blk", None),
        ),
        check_vma=False,
    )
```

```python
import functools

import jax
import jax.numpy as jnp
from jax import lax
from jax.experimental import pallas as pl
from jax.experimental.pallas import tpu as pltpu
from jax.sharding import PartitionSpec as P

NZ, NX, NC = 4, 4, 2
NY, NH = 4, 4
Y_GROUPS = [[y * NH + h for y in range(NY)] for h in range(NH)]
H_GROUPS = [[y * NH + h for h in range(NH)] for y in range(NY)]
CORE_SWAP = [(i, i ^ 1) for i in range(NZ * NX * NC)]
FLAG = 128
BF16, F32 = jnp.bfloat16, jnp.float32


def z_shift(d):
    step = NX * NC
    return [(i, (i // step + d) % NZ * step + i % step) for i in range(NZ * step)]


def x_shift(d):
    step = NX * NC
    return [(i, i // step * step + (i + d * NC) % step) for i in range(NZ * step)]


def exchange(parts, axis, perm, sign=1):
    return parts[:1] + [lax.ppermute(p, axis, perm(sign * d)) for d, p in enumerate(parts) if d]


def pieces(x, n):
    k = x.shape[0] // n
    return [x[i * k : (i + 1) * k] for i in range(n)]


def dot_t(a, b):
    return lax.dot_general(a, b, (((1,), (1,)), ((), ())), preferred_element_type=F32)


def t_dot(a, b):
    return lax.dot_general(a, b, (((0,), (0,)), ((), ())), preferred_element_type=F32)


def dot(a, b):
    return jnp.dot(a, b, preferred_element_type=F32)


def split(a):
    hi = a.astype(BF16)
    return hi, (a - hi.astype(F32)).astype(BF16)


def swap(x, members):
    return lax.all_to_all(
        x, "group", split_axis=0, concat_axis=0, axis_index_groups=members, tiled=True
    )


def turn(x, outer, inner):
    cut = pieces(x, outer * inner)
    return jnp.concatenate(
        [cut[o * inner + i] for i in range(inner) for o in range(outer)], axis=0
    )


def iota(dims, dim):
    return lax.broadcasted_iota(jnp.int32, dims, dim)


def shape(dims, dtype=BF16):
    return jax.ShapeDtypeStruct(dims, dtype)


def call(kernel, outs, args, name, flops, grant, scalars=1):
    size = sum(a.size * a.dtype.itemsize for a in (*args, *outs))
    return pl.pallas_call(
        kernel,
        in_specs=[pl.BlockSpec(memory_space=pltpu.SMEM)] * scalars
        + [pl.BlockSpec(memory_space=pltpu.VMEM)] * (len(args) - scalars),
        out_specs=[pl.BlockSpec(memory_space=pltpu.VMEM)] * len(outs),
        out_shape=outs,
        cost_estimate=pl.CostEstimate(flops=flops, bytes_accessed=size, transcendentals=0),
        compiler_params=pltpu.CompilerParams(vmem_limit_bytes=grant << 20),
        name=name,
    )(*args)


def over_columns(width, step, block=512):
    @pl.loop(0, width // block)
    def _(i):
        step(pl.ds(pl.multiple_of(i * block, block), block))


def joined(refs, cols=slice(None)):
    return jnp.concatenate([r[:, cols] for r in refs], axis=0)


def flip(x):
    n = x.shape[1]
    return dot_t((iota((n, n), 0) == iota((n, n), 1)).astype(BF16), x).astype(BF16)


def pack_kernel(groups, slots, dest_ref, rows_ref, packed_ref, placing_ref):
    dest = dest_ref[...]
    count, width = rows_ref.shape
    hot = (dest == iota((groups, count), 0)).astype(F32)
    ahead = (iota((count, count), 0) < iota((count, count), 1)).astype(F32)
    rank = jnp.sum(dot(hot, ahead) * hot, axis=0, keepdims=True).astype(jnp.int32)
    placing = (dest * slots + rank == iota((groups * slots, count), 0)).astype(BF16)
    packed_ref[:, :width] = dot(placing, rows_ref[...]).astype(BF16)
    packed_ref[:, width:] = dot(placing, jnp.ones((count, FLAG), BF16)).astype(BF16)
    placing_ref[...] = placing


def near_kernel(scale, q_ref, *refs):
    refs[-1][...] = scale * dot_t(q_ref[...], joined(refs[:-1]))


def coef_kernel(
    scale, q_ref, far0, far1, far2, far3, got_ref, s0_ref, column_ref,
    away_ref, mine_ref, hard_ref, both0_ref, both1_ref, bothh_ref, loss_ref,
):
    count, width = q_ref.shape
    q, s0 = q_ref[...], s0_ref[...]
    half = s0.shape[1]
    s1 = scale * dot_t(q, joined((far0, far1, far2, far3)))
    flags = dot_t(jnp.ones((count, FLAG), BF16), got_ref[:, width:])
    sh = jnp.where(flags > 0.5 * FLAG, scale * dot_t(q, got_ref[:, :width]), -jnp.inf)
    top = jnp.maximum(
        jnp.max(jnp.maximum(s0, s1), axis=1, keepdims=True), jnp.max(sh, axis=1, keepdims=True)
    )
    total = jnp.sum(jnp.exp(s0 - top) + jnp.exp(s1 - top), axis=1, keepdims=True)
    total = total + jnp.sum(jnp.exp(sh - top), axis=1, keepdims=True)
    log_total = top + jnp.log(total)
    column = column_ref[...]
    hot0 = column == iota((count, half), 1)
    hot1 = column == iota((count, half), 1) + half
    at_target = jnp.sum(jnp.where(hot0, s0, 0.0) + jnp.where(hot1, s1, 0.0), axis=1, keepdims=True)
    loss_ref[...] = log_total - at_target
    hi1, lo1 = split(jnp.exp(s1 - log_total) - hot1.astype(F32))
    away = flip(hi1)

    def send(cols):
        away_ref[:, cols] = dot(away, q_ref[:, cols]).astype(BF16)

    over_columns(width, send)
    both1_ref[:count], both1_ref[count:] = hi1, lo1
    hi0, lo0 = split(jnp.exp(s0 - log_total) - hot0.astype(F32))
    both0_ref[:count], both0_ref[count:] = hi0, lo0
    mine_ref[...] = flip(hi0)
    hih, loh = split(jnp.exp(sh - log_total))
    bothh_ref[:count], bothh_ref[count:] = hih, loh
    hard_ref[...] = flip(hih)


def core_sum_kernel(coef_ref, q_ref, away_ref, own_ref, *sent_refs):
    n = own_ref.shape[0]

    def add(cols):
        total = dot(coef_ref[...], q_ref[:, cols]) + away_ref[:, cols].astype(F32)
        own_ref[:, cols] = total[:n]
        for d, ref in enumerate(sent_refs):
            ref[:, cols] = total[(d + 1) * n : (d + 2) * n].astype(BF16)

    over_columns(q_ref.shape[1], add)


def query_grad_kernel(scale, c0, c1, ch, *refs):
    near, far, got, out = refs[:4], refs[4:8], refs[8], refs[9]
    count = out.shape[1]

    def grad(cols):
        both = dot(c0[...], joined(near, cols)) + dot(c1[...], joined(far, cols))
        both = both + dot(ch[...], got[:, cols])
        out[0, :, cols] = (scale * (both[:count] + both[count:])).astype(out.dtype)

    over_columns(out.shape[2], grad)


def body(queries, passages, positives, hard_rows, hard_dest):
    q = queries[0]
    own = passages[0]
    targets = positives[0]
    owned_hard = hard_rows[0]
    count, width = q.shape
    rows = own.shape[0]
    groups = NY * NH
    slots = max(2, 2 * owned_hard.shape[0] // groups)
    half, places = NZ * NX * rows, groups * slots
    scale = width ** (-0.5)
    blk = lax.axis_index("blk")
    my_z, my_x, my_c = blk // (NX * NC), blk // NC % NX, blk % NC

    with jax.named_scope("gather_z"):
        z_rows = jnp.concatenate(exchange([own] * NZ, "blk", z_shift), axis=0)
    with jax.named_scope("hard_out"):
        packed, placing = call(
            functools.partial(pack_kernel, groups, slots),
            [shape((places, width + FLAG)), shape((places, owned_hard.shape[0]))],
            (hard_dest.reshape(1, -1), owned_hard),
            "pack", 2 * places * owned_hard.size, 2, 0,
        )
        from_y = swap(packed, Y_GROUPS)
        received = swap(turn(from_y, NY, NH), H_GROUPS)
    with jax.named_scope("gather_x"):
        last, _ = lax.optimization_barrier((z_rows, from_y))
        near = exchange([z_rows] * (NX - 1) + [last], "blk", x_shift)
    with jax.named_scope("gather_core"):
        far = [lax.ppermute(x, "blk", CORE_SWAP) for x in near]

    owner = targets // rows
    o_z, o_x, o_c = owner // (NX * NC), owner // NC % NX, owner % NC
    column = (
        (o_c != my_c).astype(jnp.int32) * half
        + ((my_x - o_x) % NX * NZ + (my_z - o_z) % NZ) * rows
        + targets % rows
    )
    with jax.named_scope("scores"):
        [s0] = call(
            functools.partial(near_kernel, scale),
            [shape((count, half), F32)],
            (q, *near),
            "near", 2 * count * half * width, 8, 0,
        )
        away, mine_rows, hard_cols, both0, both1, both_hard, loss_rows = call(
            functools.partial(coef_kernel, scale),
            [
                shape((half, width)), shape((half, count)), shape((places, count)),
                shape((2 * count, half)), shape((2 * count, half)), shape((2 * count, places)),
                shape((count, 1), F32),
            ],
            (q, *far, received, s0, column.reshape(-1, 1)),
            "coef", 4 * count * half * width, 12, 0,
        )
    with jax.named_scope("scatter_core"):
        away = lax.ppermute(away, "blk", CORE_SWAP)
    with jax.named_scope("scatter_x"):
        n = half // NX
        mine = call(
            core_sum_kernel,
            [shape((n, width), F32)] + [shape((n, width))] * (NX - 1),
            (mine_rows, q, away),
            "core_sum", 2 * count * half * width, 8, 0,
        )
        chunks = [c.astype(F32) for c in exchange(list(mine), "blk", x_shift, -1)]
        mine_x = pieces(functools.reduce(jnp.add, chunks), NZ)

    hard_cols, both0, _ = lax.optimization_barrier((hard_cols, both0, away))
    with jax.named_scope("hard_back"):
        g = (scale * dot(hard_cols, q)).astype(BF16)
        returned = swap(turn(swap(g, H_GROUPS), NH, NY), Y_GROUPS)
        d_owned = t_dot(placing, returned).astype(BF16)
    with jax.named_scope("d_query"):
        [d_query] = call(
            functools.partial(query_grad_kernel, scale),
            [shape((1, count, width))],
            (both0, both1, both_hard, *near, *far, received),
            "query_grad", 4 * count * (2 * half + places) * width, 8, 0,
        )
    with jax.named_scope("scatter_z"):
        sent = [mine_x[0]] + [m.astype(BF16) for m in mine_x[1:]]
        chunks = [c.astype(F32) for c in exchange(sent, "blk", z_shift, -1)]
        d_passage = (scale * functools.reduce(jnp.add, chunks)).astype(BF16)
    return (loss_rows.reshape(1, -1), d_query, d_passage[None], d_owned[None])


def solution(mesh):
    return jax.shard_map(
        body,
        mesh=mesh,
        in_specs=(
            P("group", "blk", None),
            P("group", "blk", None),
            P("group", "blk"),
            P("group", "blk", None),
            P("group", "blk", None),
        ),
        out_specs=(
            P("group", "blk"),
            P("group", "blk", None),
            P("group", "blk", None),
            P("group", "blk", None),
        ),
        check_vma=False,
    )
```

```python
import functools

import jax
import jax.numpy as jnp
from jax import lax
from jax.experimental import pallas as pl
from jax.experimental.pallas import tpu as pltpu
from jax.sharding import PartitionSpec as P

NZ, NX, NC = 4, 4, 2
NY, NH = 4, 4
Y_GROUPS = [[y * NH + h for y in range(NY)] for h in range(NH)]
H_GROUPS = [[y * NH + h for h in range(NH)] for y in range(NY)]
CORE_SWAP = [(i, i ^ 1) for i in range(NZ * NX * NC)]
FLAG = 128
BF16, F32 = jnp.bfloat16, jnp.float32


def z_shift(d):
    step = NX * NC
    return [(i, (i // step + d) % NZ * step + i % step) for i in range(NZ * step)]


def x_shift(d):
    step = NX * NC
    return [(i, i // step * step + (i + d * NC) % step) for i in range(NZ * step)]


def exchange(parts, axis, perm, sign=1):
    return parts[:1] + [lax.ppermute(p, axis, perm(sign * d)) for d, p in enumerate(parts) if d]


def pieces(x, n):
    k = x.shape[0] // n
    return [x[i * k : (i + 1) * k] for i in range(n)]


def dot_t(a, b):
    return lax.dot_general(a, b, (((1,), (1,)), ((), ())), preferred_element_type=F32)


def t_dot(a, b):
    return lax.dot_general(a, b, (((0,), (0,)), ((), ())), preferred_element_type=F32)


def dot(a, b):
    return jnp.dot(a, b, preferred_element_type=F32)


def split(a):
    hi = a.astype(BF16)
    return hi, (a - hi.astype(F32)).astype(BF16)


def swap(x, members):
    return lax.all_to_all(
        x, "group", split_axis=0, concat_axis=0, axis_index_groups=members, tiled=True
    )


def iota(dims, dim):
    return lax.broadcasted_iota(jnp.int32, dims, dim)


def shape(dims, dtype=BF16):
    return jax.ShapeDtypeStruct(dims, dtype)


def call(kernel, outs, args, name, flops, grant, scalars=1):
    size = sum(a.size * a.dtype.itemsize for a in (*args, *outs))
    return pl.pallas_call(
        kernel,
        in_specs=[pl.BlockSpec(memory_space=pltpu.SMEM)] * scalars
        + [pl.BlockSpec(memory_space=pltpu.VMEM)] * (len(args) - scalars),
        out_specs=[pl.BlockSpec(memory_space=pltpu.VMEM)] * len(outs),
        out_shape=outs,
        cost_estimate=pl.CostEstimate(flops=flops, bytes_accessed=size, transcendentals=0),
        compiler_params=pltpu.CompilerParams(vmem_limit_bytes=grant << 20),
        name=name,
    )(*args)


def over_columns(width, step, block=512):
    @pl.loop(0, width // block)
    def _(i):
        step(pl.ds(pl.multiple_of(i * block, block), block))


def joined(refs, cols=slice(None)):
    return jnp.concatenate([r[:, cols] for r in refs], axis=0)


def flip(x, pick=None):
    n = x.shape[1]
    pick = iota((n, n), 0) == iota((n, n), 1) if pick is None else pick
    return dot_t(pick.astype(BF16), x).astype(BF16)


def swapped(n, slots):
    row, col = iota((n, n), 0), iota((n, n), 1)
    place = row // slots
    return (place % NH * NY + place // NH) * slots + row % slots == col


def turn_kernel(slots, in_ref, out_ref):
    pick = swapped(in_ref.shape[0], slots).astype(BF16)
    out_ref[...] = dot(pick, in_ref[...]).astype(BF16)


def turn(x, slots):
    [out] = call(
        functools.partial(turn_kernel, slots), [shape(x.shape)], (x,),
        "turn", 2 * x.shape[0] * x.size, 2, 0,
    )
    return out


def pack_kernel(slots, dest_ref, rows_ref, packed_ref, placing_ref):
    dest = dest_ref[...]
    count, width = rows_ref.shape
    groups = NY * NH
    hot = (dest == iota((groups, count), 0)).astype(F32)
    ahead = (iota((count, count), 0) < iota((count, count), 1)).astype(F32)
    rank = jnp.sum(dot(hot, ahead) * hot, axis=0, keepdims=True).astype(jnp.int32)
    at = iota((groups * slots, count), 0)
    send = (dest * slots + rank == at).astype(BF16)
    packed_ref[:, :width] = dot(send, rows_ref[...]).astype(BF16)
    packed_ref[:, width:] = dot(send, jnp.ones((count, FLAG), BF16)).astype(BF16)
    placing_ref[...] = ((dest % NH * NY + dest // NH) * slots + rank == at).astype(BF16)


def near_kernel(scale, q_ref, *refs):
    refs[-1][...] = scale * dot_t(q_ref[...], joined(refs[:-1]))


def hot(column_ref, dims, start):
    return column_ref[...] == iota(dims, 1) + start


def away_kernel(
    scale, q_ref, far0, far1, far2, far3, got_ref, s0_ref, column_ref,
    first_ref, second_ref, s1_ref, sh_ref, log_ref,
):
    count, width = q_ref.shape
    q, s0 = q_ref[...], s0_ref[...]
    half = s0.shape[1]
    flags = dot_t(jnp.ones((count, FLAG), BF16), got_ref[:, width:])
    sh = jnp.where(flags > 0.5 * FLAG, scale * dot_t(q, got_ref[:, :width]), -jnp.inf)
    s1 = scale * dot_t(q, joined((far0, far1, far2, far3)))
    top = jnp.maximum(
        jnp.max(jnp.maximum(s0, s1), axis=1, keepdims=True), jnp.max(sh, axis=1, keepdims=True)
    )
    total = jnp.sum(jnp.exp(s0 - top) + jnp.exp(s1 - top), axis=1, keepdims=True)
    total = total + jnp.sum(jnp.exp(sh - top), axis=1, keepdims=True)
    log_total = top + jnp.log(total)
    c1 = jnp.exp(s1 - log_total) - hot(column_ref, (count, half), half).astype(F32)
    away = flip(c1.astype(BF16))
    n = half // NX

    def send(cols):
        rows = dot(away, q_ref[:, cols]).astype(BF16)
        first_ref[:, cols] = rows[n : 3 * n]
        second_ref[:n, cols], second_ref[n:, cols] = rows[:n], rows[3 * n :]

    over_columns(width, send)
    s1_ref[...], sh_ref[...], log_ref[...] = s1, sh, log_total


def coef_kernel(
    slots, s0_ref, s1_ref, sh_ref, log_ref, column_ref,
    mine_ref, hard_ref, both0_ref, both1_ref, bothh_ref, loss_ref,
):
    s0, s1, log_total = s0_ref[...], s1_ref[...], log_ref[...]
    count, half = s0.shape
    hot0, hot1 = hot(column_ref, s0.shape, 0), hot(column_ref, s0.shape, half)
    hi0, lo0 = split(jnp.exp(s0 - log_total) - hot0.astype(F32))
    mine_ref[...] = flip(hi0)
    both0_ref[:count], both0_ref[count:] = hi0, lo0
    hih, loh = split(jnp.exp(sh_ref[...] - log_total))
    hard_ref[...] = flip(hih, swapped(hih.shape[1], slots))
    bothh_ref[:count], bothh_ref[count:] = hih, loh
    hi1, lo1 = split(jnp.exp(s1 - log_total) - hot1.astype(F32))
    both1_ref[:count], both1_ref[count:] = hi1, lo1
    at_target = jnp.sum(jnp.where(hot0, s0, 0.0) + jnp.where(hot1, s1, 0.0), axis=1, keepdims=True)
    loss_ref[...] = log_total - at_target


def core_sum_kernel(first, coef_ref, q_ref, away_ref, *out_refs):
    n = out_refs[0].shape[0]
    coef = coef_ref[...]
    coef = coef[n : 3 * n] if first else jnp.concatenate([coef[:n], coef[3 * n :]], axis=0)

    def add(cols):
        total = dot(coef, q_ref[:, cols]) + away_ref[:, cols].astype(F32)
        for i, ref in enumerate(out_refs):
            ref[:, cols] = total[i * n : (i + 1) * n].astype(ref.dtype)

    over_columns(q_ref.shape[1], add)


def query_grad_kernel(scale, c0, c1, ch, *refs):
    near, far, got, out = refs[:4], refs[4:8], refs[8], refs[9]
    count = out.shape[1]

    def grad(cols):
        both = dot(c0[...], joined(near, cols)) + dot(c1[...], joined(far, cols))
        both = both + dot(ch[...], got[:, cols])
        out[0, :, cols] = (scale * (both[:count] + both[count:])).astype(out.dtype)

    over_columns(out.shape[2], grad)


def body(queries, passages, positives, hard_rows, hard_dest):
    q = queries[0]
    own = passages[0]
    targets = positives[0]
    owned_hard = hard_rows[0]
    count, width = q.shape
    rows = own.shape[0]
    groups = NY * NH
    slots = max(2, 2 * owned_hard.shape[0] // groups)
    half, places = NZ * NX * rows, groups * slots
    scale = width ** (-0.5)
    blk = lax.axis_index("blk")
    my_z, my_x, my_c = blk // (NX * NC), blk // NC % NX, blk % NC

    with jax.named_scope("gather_z"):
        z_rows = jnp.concatenate(exchange([own] * NZ, "blk", z_shift), axis=0)
    with jax.named_scope("hard_out"):
        packed, placing = call(
            functools.partial(pack_kernel, slots),
            [shape((places, width + FLAG)), shape((places, owned_hard.shape[0]))],
            (hard_dest.reshape(1, -1), owned_hard),
            "pack", 2 * places * owned_hard.size, 2, 0,
        )
        from_y = swap(packed, Y_GROUPS)
        received = swap(turn(from_y, slots), H_GROUPS)
    with jax.named_scope("gather_x"):
        last, _ = lax.optimization_barrier((z_rows, from_y))
        near = exchange([z_rows] * (NX - 1) + [last], "blk", x_shift)
    with jax.named_scope("gather_core"):
        far = [lax.ppermute(x, "blk", CORE_SWAP) for x in near]

    owner = targets // rows
    o_z, o_x, o_c = owner // (NX * NC), owner // NC % NX, owner % NC
    column = (
        (o_c != my_c).astype(jnp.int32) * half
        + ((my_x - o_x) % NX * NZ + (my_z - o_z) % NZ) * rows
        + targets % rows
    )
    with jax.named_scope("scores"):
        [s0] = call(
            functools.partial(near_kernel, scale),
            [shape((count, half), F32)],
            (q, *near),
            "near", 2 * count * half * width, 8, 0,
        )
        first, second, s1, sh, log_total = call(
            functools.partial(away_kernel, scale),
            [
                shape((half // 2, width)), shape((half // 2, width)), shape((count, half), F32),
                shape((count, places), F32), shape((count, 1), F32),
            ],
            (q, *far, received, s0, column.reshape(-1, 1)),
            "away", 4 * count * half * width, 12, 0,
        )
        mine_rows, hard_cols, both0, both1, both_hard, loss_rows = call(
            functools.partial(coef_kernel, slots),
            [
                shape((half, count)), shape((places, count)), shape((2 * count, half)),
                shape((2 * count, half)), shape((2 * count, places)), shape((count, 1), F32),
            ],
            (s0, s1, sh, log_total, column.reshape(-1, 1)),
            "coef", count * half * half, 8, 0,
        )
    with jax.named_scope("scatter_core"):
        first = lax.ppermute(first, "blk", CORE_SWAP)
        second = lax.ppermute(second, "blk", CORE_SWAP)
    with jax.named_scope("scatter_x"):
        n = half // NX
        flops = count * half * width
        one, two = call(
            functools.partial(core_sum_kernel, True), [shape((n, width))] * 2,
            (mine_rows, q, first), "core_sum_first", flops, 8, 0,
        )
        zero, three = call(
            functools.partial(core_sum_kernel, False), [shape((n, width), F32), shape((n, width))],
            (mine_rows, q, second), "core_sum_second", flops, 8, 0,
        )
        chunks = [c.astype(F32) for c in exchange([zero, one, two, three], "blk", x_shift, -1)]
        mine_x = pieces(functools.reduce(jnp.add, chunks), NZ)

    hard_cols, _ = lax.optimization_barrier((hard_cols, second))
    with jax.named_scope("hard_back"):
        g = (scale * dot(hard_cols, q)).astype(BF16)
        back = turn(swap(g, Y_GROUPS), slots)
        returned = swap(back, H_GROUPS)
        d_owned = t_dot(placing, returned).astype(BF16)
    both0, _ = lax.optimization_barrier((both0, back))
    with jax.named_scope("d_query"):
        [d_query] = call(
            functools.partial(query_grad_kernel, scale),
            [shape((1, count, width))],
            (both0, both1, both_hard, *near, *far, received),
            "query_grad", 4 * count * (2 * half + places) * width, 8, 0,
        )
    with jax.named_scope("scatter_z"):
        sent = [mine_x[0]] + [m.astype(BF16) for m in mine_x[1:]]
        chunks = [c.astype(F32) for c in exchange(sent, "blk", z_shift, -1)]
        d_passage = (scale * functools.reduce(jnp.add, chunks)).astype(BF16)
    return (loss_rows.reshape(1, -1), d_query, d_passage[None], d_owned[None])


def solution(mesh):
    return jax.shard_map(
        body,
        mesh=mesh,
        in_specs=(
            P("group", "blk", None),
            P("group", "blk", None),
            P("group", "blk"),
            P("group", "blk", None),
            P("group", "blk", None),
        ),
        out_specs=(
            P("group", "blk"),
            P("group", "blk", None),
            P("group", "blk", None),
            P("group", "blk", None),
        ),
        check_vma=False,
    )
```

```python
import functools

import jax
import jax.numpy as jnp
from jax import lax
from jax.experimental import pallas as pl
from jax.experimental.pallas import tpu as pltpu
from jax.sharding import PartitionSpec as P

NZ, NX, NC = 4, 4, 2
NY, NH = 4, 4
Y_GROUPS = [[y * NH + h for y in range(NY)] for h in range(NH)]
H_GROUPS = [[y * NH + h for h in range(NH)] for y in range(NY)]
CORE_SWAP = [(i, i ^ 1) for i in range(NZ * NX * NC)]
FLAG = 128
BF16, F32 = jnp.bfloat16, jnp.float32


def z_shift(d):
    step = NX * NC
    return [(i, (i // step + d) % NZ * step + i % step) for i in range(NZ * step)]


def x_shift(d):
    step = NX * NC
    return [(i, i // step * step + (i + d * NC) % step) for i in range(NZ * step)]


def exchange(parts, axis, perm, sign=1):
    return parts[:1] + [lax.ppermute(p, axis, perm(sign * d)) for d, p in enumerate(parts) if d]


def pieces(x, n):
    k = x.shape[0] // n
    return [x[i * k : (i + 1) * k] for i in range(n)]


def dot_t(a, b):
    return lax.dot_general(a, b, (((1,), (1,)), ((), ())), preferred_element_type=F32)


def t_dot(a, b):
    return lax.dot_general(a, b, (((0,), (0,)), ((), ())), preferred_element_type=F32)


def dot(a, b):
    return jnp.dot(a, b, preferred_element_type=F32)


def split(a):
    hi = a.astype(BF16)
    return hi, (a - hi.astype(F32)).astype(BF16)


def swap(x, members):
    return lax.all_to_all(
        x, "group", split_axis=0, concat_axis=0, axis_index_groups=members, tiled=True
    )


def iota(dims, dim):
    return lax.broadcasted_iota(jnp.int32, dims, dim)


def shape(dims, dtype=BF16):
    return jax.ShapeDtypeStruct(dims, dtype)


def call(kernel, outs, args, name, flops, grant, scalars=1):
    size = sum(a.size * a.dtype.itemsize for a in (*args, *outs))
    return pl.pallas_call(
        kernel,
        in_specs=[pl.BlockSpec(memory_space=pltpu.SMEM)] * scalars
        + [pl.BlockSpec(memory_space=pltpu.VMEM)] * (len(args) - scalars),
        out_specs=[pl.BlockSpec(memory_space=pltpu.VMEM)] * len(outs),
        out_shape=outs,
        cost_estimate=pl.CostEstimate(flops=flops, bytes_accessed=size, transcendentals=0),
        compiler_params=pltpu.CompilerParams(vmem_limit_bytes=grant << 20),
        name=name,
    )(*args)


def over_columns(width, step, block=512):
    @pl.loop(0, width // block)
    def _(i):
        step(pl.ds(pl.multiple_of(i * block, block), block))


def joined(refs, cols=slice(None)):
    return jnp.concatenate([r[:, cols] for r in refs], axis=0)


def flip(x, pick=None):
    n = x.shape[1]
    pick = iota((n, n), 0) == iota((n, n), 1) if pick is None else pick
    return dot_t(pick.astype(BF16), x).astype(BF16)


def swapped(n, slots):
    row, col = iota((n, n), 0), iota((n, n), 1)
    place = row // slots
    return (place % NH * NY + place // NH) * slots + row % slots == col


def turn_kernel(slots, in_ref, out_ref):
    pick = swapped(in_ref.shape[0], slots).astype(BF16)
    out_ref[...] = dot(pick, in_ref[...]).astype(BF16)


def turn(x, slots):
    [out] = call(
        functools.partial(turn_kernel, slots), [shape(x.shape)], (x,),
        "turn", 2 * x.shape[0] * x.size, 2, 0,
    )
    return out


def pack_kernel(slots, dest_ref, rows_ref, packed_ref, placing_ref):
    dest = dest_ref[...]
    count, width = rows_ref.shape
    groups = NY * NH
    hot = (dest == iota((groups, count), 0)).astype(F32)
    ahead = (iota((count, count), 0) < iota((count, count), 1)).astype(F32)
    rank = jnp.sum(dot(hot, ahead) * hot, axis=0, keepdims=True).astype(jnp.int32)
    at = iota((groups * slots, count), 0)
    send = (dest * slots + rank == at).astype(BF16)
    packed_ref[:, :width] = dot(send, rows_ref[...]).astype(BF16)
    packed_ref[:, width:] = dot(send, jnp.ones((count, FLAG), BF16)).astype(BF16)
    placing_ref[...] = send


def near_kernel(scale, q_ref, *refs):
    refs[-1][...] = scale * dot_t(q_ref[...], joined(refs[:-1]))


def hot(column_ref, dims, start):
    return column_ref[...] == iota(dims, 1) + start


def away_kernel(
    scale, q_ref, far0, far1, far2, far3, got_ref, s0_ref, column_ref,
    first_ref, second_ref, s1_ref, sh_ref, log_ref,
):
    count, width = q_ref.shape
    q, s0 = q_ref[...], s0_ref[...]
    half = s0.shape[1]
    flags = dot_t(jnp.ones((count, FLAG), BF16), got_ref[:, width:])
    sh = jnp.where(flags > 0.5 * FLAG, scale * dot_t(q, got_ref[:, :width]), -jnp.inf)
    s1 = scale * dot_t(q, joined((far0, far1, far2, far3)))
    top = jnp.maximum(
        jnp.max(jnp.maximum(s0, s1), axis=1, keepdims=True), jnp.max(sh, axis=1, keepdims=True)
    )
    total = jnp.sum(jnp.exp(s0 - top) + jnp.exp(s1 - top), axis=1, keepdims=True)
    total = total + jnp.sum(jnp.exp(sh - top), axis=1, keepdims=True)
    log_total = top + jnp.log(total)
    c1 = jnp.exp(s1 - log_total) - hot(column_ref, (count, half), half).astype(F32)
    away = flip(c1.astype(BF16))
    n = half // NX

    def send(cols):
        rows = dot(away, q_ref[:, cols]).astype(BF16)
        first_ref[:, cols] = rows[n : 3 * n]
        second_ref[:n, cols], second_ref[n:, cols] = rows[:n], rows[3 * n :]

    over_columns(width, send)
    s1_ref[...], sh_ref[...], log_ref[...] = s1, sh, log_total


def coef_kernel(
    slots, s0_ref, s1_ref, sh_ref, log_ref, column_ref,
    mine_ref, hard_ref, both0_ref, both1_ref, bothh_ref, loss_ref,
):
    s0, s1, log_total = s0_ref[...], s1_ref[...], log_ref[...]
    count, half = s0.shape
    hot0, hot1 = hot(column_ref, s0.shape, 0), hot(column_ref, s0.shape, half)
    hi0, lo0 = split(jnp.exp(s0 - log_total) - hot0.astype(F32))
    mine_ref[...] = flip(hi0)
    both0_ref[:count], both0_ref[count:] = hi0, lo0
    hih, loh = split(jnp.exp(sh_ref[...] - log_total))
    hard_ref[...] = flip(hih, swapped(hih.shape[1], slots))
    bothh_ref[...] = jnp.concatenate([hih, loh], axis=1)
    hi1, lo1 = split(jnp.exp(s1 - log_total) - hot1.astype(F32))
    both1_ref[:count], both1_ref[count:] = hi1, lo1
    at_target = jnp.sum(jnp.where(hot0, s0, 0.0) + jnp.where(hot1, s1, 0.0), axis=1, keepdims=True)
    loss_ref[...] = log_total - at_target


def core_sum_kernel(first, coef_ref, q_ref, away_ref, *out_refs):
    n = out_refs[0].shape[0]
    coef = coef_ref[...]
    coef = coef[n : 3 * n] if first else jnp.concatenate([coef[:n], coef[3 * n :]], axis=0)

    def add(cols):
        total = dot(coef, q_ref[:, cols]) + away_ref[:, cols].astype(F32)
        for i, ref in enumerate(out_refs):
            ref[:, cols] = total[i * n : (i + 1) * n].astype(ref.dtype)

    over_columns(q_ref.shape[1], add)


def hard_grad_kernel(scale, coef_ref, q_ref, out_ref):
    places, slots, width = out_ref.shape

    def grad(cols):
        rows = scale * dot(coef_ref[...], q_ref[:, cols])
        for i in range(places):
            out_ref[i, :, cols] = rows[i * slots : (i + 1) * slots].astype(out_ref.dtype)

    over_columns(width, grad)


def query_grad_kernel(scale, c0, c1, ch, *refs):
    near, far, got, out = refs[:4], refs[4:8], refs[8], refs[9]
    count = out.shape[1]

    def grad(cols):
        both = dot(c0[...], joined(near, cols)) + dot(c1[...], joined(far, cols))
        hard = got[:, cols]
        thin = dot(ch[...], jnp.concatenate([hard, hard], axis=0))
        out[0, :, cols] = (scale * (both[:count] + both[count:] + thin)).astype(out.dtype)

    over_columns(out.shape[2], grad)


def body(queries, passages, positives, hard_rows, hard_dest):
    q = queries[0]
    own = passages[0]
    targets = positives[0]
    owned_hard = hard_rows[0]
    count, width = q.shape
    rows = own.shape[0]
    groups = NY * NH
    slots = max(2, 2 * owned_hard.shape[0] // groups)
    half, places = NZ * NX * rows, groups * slots
    scale = width ** (-0.5)
    blk = lax.axis_index("blk")
    my_z, my_x, my_c = blk // (NX * NC), blk // NC % NX, blk % NC

    with jax.named_scope("gather_z"):
        z_rows = jnp.concatenate(exchange([own] * NZ, "blk", z_shift), axis=0)
    with jax.named_scope("hard_out"):
        packed, placing = call(
            functools.partial(pack_kernel, slots),
            [shape((places, width + FLAG)), shape((places, owned_hard.shape[0]))],
            (hard_dest.reshape(1, -1), owned_hard),
            "pack", 2 * places * owned_hard.size, 2, 0,
        )
        from_y = swap(packed, Y_GROUPS)
        received = swap(turn(from_y, slots), H_GROUPS)
    with jax.named_scope("gather_x"):
        last, _ = lax.optimization_barrier((z_rows, from_y))
        near = exchange([z_rows] * (NX - 1) + [last], "blk", x_shift)
    with jax.named_scope("gather_core"):
        far = [lax.ppermute(x, "blk", CORE_SWAP) for x in near]

    owner = targets // rows
    o_z, o_x, o_c = owner // (NX * NC), owner // NC % NX, owner % NC
    column = (
        (o_c != my_c).astype(jnp.int32) * half
        + ((my_x - o_x) % NX * NZ + (my_z - o_z) % NZ) * rows
        + targets % rows
    )
    with jax.named_scope("scores"):
        [s0] = call(
            functools.partial(near_kernel, scale),
            [shape((count, half), F32)],
            (q, *near),
            "near", 2 * count * half * width, 8, 0,
        )
        first, second, s1, sh, log_total = call(
            functools.partial(away_kernel, scale),
            [
                shape((half // 2, width)), shape((half // 2, width)), shape((count, half), F32),
                shape((count, places), F32), shape((count, 1), F32),
            ],
            (q, *far, received, s0, column.reshape(-1, 1)),
            "away", 4 * count * half * width, 12, 0,
        )
        mine_rows, hard_cols, both0, both1, both_hard, loss_rows = call(
            functools.partial(coef_kernel, slots),
            [
                shape((half, count)), shape((places, count)), shape((2 * count, half)),
                shape((2 * count, half)), shape((count, 2 * places)), shape((count, 1), F32),
            ],
            (s0, s1, sh, log_total, column.reshape(-1, 1)),
            "coef", count * half * half, 8, 0,
        )
    with jax.named_scope("scatter_core"):
        first = lax.ppermute(first, "blk", CORE_SWAP)
        second = lax.ppermute(second, "blk", CORE_SWAP)
    with jax.named_scope("scatter_x"):
        n = half // NX
        flops = count * half * width
        one, two = call(
            functools.partial(core_sum_kernel, True), [shape((n, width))] * 2,
            (mine_rows, q, first), "core_sum_first", flops, 8, 0,
        )
        zero, three = call(
            functools.partial(core_sum_kernel, False), [shape((n, width), F32), shape((n, width))],
            (mine_rows, q, second), "core_sum_second", flops, 8, 0,
        )
        chunks = [c.astype(F32) for c in exchange([zero, one, two, three], "blk", x_shift, -1)]
        mine_x = pieces(functools.reduce(jnp.add, chunks), NZ)

    hard_cols, _ = lax.optimization_barrier((hard_cols, second))
    with jax.named_scope("hard_back"):
        [g] = call(
            functools.partial(hard_grad_kernel, scale), [shape((groups, slots, width))],
            (hard_cols, q), "hard_grad", 2 * places * count * width, 4, 0,
        )
        returned = lax.all_to_all(g, "group", split_axis=0, concat_axis=0, tiled=True)
        d_owned = t_dot(placing, returned.reshape(places, width)).astype(BF16)
    both0, _ = lax.optimization_barrier((both0, g))
    with jax.named_scope("d_query"):
        [d_query] = call(
            functools.partial(query_grad_kernel, scale),
            [shape((1, count, width))],
            (both0, both1, both_hard, *near, *far, received),
            "query_grad", 4 * count * (2 * half + places) * width, 8, 0,
        )
    with jax.named_scope("scatter_z"):
        sent = [mine_x[0]] + [m.astype(BF16) for m in mine_x[1:]]
        chunks = [c.astype(F32) for c in exchange(sent, "blk", z_shift, -1)]
        d_passage = (scale * functools.reduce(jnp.add, chunks)).astype(BF16)
    return (loss_rows.reshape(1, -1), d_query, d_passage[None], d_owned[None])


def solution(mesh):
    return jax.shard_map(
        body,
        mesh=mesh,
        in_specs=(
            P("group", "blk", None),
            P("group", "blk", None),
            P("group", "blk"),
            P("group", "blk", None),
            P("group", "blk", None),
        ),
        out_specs=(
            P("group", "blk"),
            P("group", "blk", None),
            P("group", "blk", None),
            P("group", "blk", None),
        ),
        check_vma=False,
    )
```

```python
import functools

import jax
import jax.numpy as jnp
from jax import lax
from jax.experimental import pallas as pl
from jax.experimental.pallas import tpu as pltpu
from jax.sharding import PartitionSpec as P

NZ, NX, NC = 4, 4, 2
NY, NH = 4, 4
Y_GROUPS = [[y * NH + h for y in range(NY)] for h in range(NH)]
H_GROUPS = [[y * NH + h for h in range(NH)] for y in range(NY)]
CORE_SWAP = [(i, i ^ 1) for i in range(NZ * NX * NC)]
FLAG = 128
BF16, F32 = jnp.bfloat16, jnp.float32


def z_shift(d):
    step = NX * NC
    return [(i, (i // step + d) % NZ * step + i % step) for i in range(NZ * step)]


def x_shift(d):
    step = NX * NC
    return [(i, i // step * step + (i + d * NC) % step) for i in range(NZ * step)]


def exchange(parts, axis, perm, sign=1):
    return parts[:1] + [lax.ppermute(p, axis, perm(sign * d)) for d, p in enumerate(parts) if d]


def pieces(x, n):
    k = x.shape[0] // n
    return [x[i * k : (i + 1) * k] for i in range(n)]


def dot_t(a, b):
    return lax.dot_general(a, b, (((1,), (1,)), ((), ())), preferred_element_type=F32)


def t_dot(a, b):
    return lax.dot_general(a, b, (((0,), (0,)), ((), ())), preferred_element_type=F32)


def dot(a, b):
    return jnp.dot(a, b, preferred_element_type=F32)


def split(a):
    hi = a.astype(BF16)
    return hi, (a - hi.astype(F32)).astype(BF16)


def swap(x, members):
    return lax.all_to_all(
        x, "group", split_axis=0, concat_axis=0, axis_index_groups=members, tiled=True
    )


def iota(dims, dim):
    return lax.broadcasted_iota(jnp.int32, dims, dim)


def shape(dims, dtype=BF16):
    return jax.ShapeDtypeStruct(dims, dtype)


def call(kernel, outs, args, name, flops, grant, place=pltpu.VMEM, scratch=()):
    size = sum(a.size * a.dtype.itemsize for a in (*args, *outs))
    return pl.pallas_call(
        kernel,
        in_specs=[pl.BlockSpec(memory_space=pltpu.VMEM)] * len(args),
        out_specs=[pl.BlockSpec(memory_space=place)] * len(outs),
        out_shape=outs,
        scratch_shapes=scratch,
        cost_estimate=pl.CostEstimate(flops=flops, bytes_accessed=size, transcendentals=0),
        compiler_params=pltpu.CompilerParams(vmem_limit_bytes=grant << 20),
        name=name,
    )(*args)


def over_columns(width, step, block=1024):
    for i in range(0, width, block):
        step(slice(i, i + block))


def joined(refs, cols=slice(None)):
    return jnp.concatenate([r[:, cols] for r in refs], axis=0)


def flip(x, pick=None):
    n = x.shape[1]
    pick = iota((n, n), 0) == iota((n, n), 1) if pick is None else pick
    return dot_t(pick.astype(BF16), x).astype(BF16)


def swapped(n, slots):
    row, col = iota((n, n), 0), iota((n, n), 1)
    place = row // slots
    return (place % NH * NY + place // NH) * slots + row % slots == col


def turn_kernel(slots, in_ref, out_ref):
    pick = swapped(in_ref.shape[0], slots).astype(BF16)
    out_ref[...] = dot(pick, in_ref[...]).astype(BF16)


def turn(x, slots):
    [out] = call(
        functools.partial(turn_kernel, slots), [shape(x.shape)], (x,),
        "turn", 2 * x.shape[0] * x.size, 2,
    )
    return out


def pack_kernel(slots, dest_ref, rows_ref, packed_ref, placing_ref):
    dest = dest_ref[...]
    count, width = rows_ref.shape
    groups = NY * NH
    hot = (dest == iota((groups, count), 0)).astype(F32)
    ahead = (iota((count, count), 0) < iota((count, count), 1)).astype(F32)
    rank = jnp.sum(dot(hot, ahead) * hot, axis=0, keepdims=True).astype(jnp.int32)
    at = iota((groups * slots, count), 0)
    send = (dest * slots + rank == at).astype(BF16)
    packed_ref[:, :width] = dot(send, rows_ref[...]).astype(BF16)
    packed_ref[:, width:] = dot(send, jnp.ones((count, FLAG), BF16)).astype(BF16)
    placing_ref[...] = send


def near_kernel(scale, q_ref, *refs):
    refs[-1][...] = scale * dot_t(q_ref[...], joined(refs[:-1]))


def hot(column_ref, dims, start):
    return column_ref[...] == iota(dims, 1) + start


def away_kernel(
    scale, q_ref, far0, far1, far2, far3, got_ref, s0_ref, column_ref,
    first_ref, second_ref, s1_ref, sh_ref, log_ref,
):
    count, width = q_ref.shape
    q, s0 = q_ref[...], s0_ref[...]
    half = s0.shape[1]
    flags = dot_t(jnp.ones((count, FLAG), BF16), got_ref[:, width:])
    sh = jnp.where(flags > 0.5 * FLAG, scale * dot_t(q, got_ref[:, :width]), -jnp.inf)
    s1 = scale * dot_t(q, joined((far0, far1, far2, far3)))
    top = jnp.maximum(
        jnp.max(jnp.maximum(s0, s1), axis=1, keepdims=True), jnp.max(sh, axis=1, keepdims=True)
    )
    total = jnp.sum(jnp.exp(s0 - top) + jnp.exp(s1 - top), axis=1, keepdims=True)
    total = total + jnp.sum(jnp.exp(sh - top), axis=1, keepdims=True)
    log_total = top + jnp.log(total)
    c1 = jnp.exp(s1 - log_total) - hot(column_ref, (count, half), half).astype(F32)
    away = flip(c1.astype(BF16))
    n = half // NX

    def send(cols):
        rows = dot(away, q_ref[:, cols]).astype(BF16)
        first_ref[:, cols] = rows[n : 3 * n]
        second_ref[:n, cols], second_ref[n:, cols] = rows[:n], rows[3 * n :]

    over_columns(width, send)
    s1_ref[...], sh_ref[...], log_ref[...] = s1, sh, log_total


def coef_kernel(
    slots, s0_ref, s1_ref, sh_ref, log_ref, column_ref,
    mine_ref, hard_ref, both0_ref, both1_ref, bothh_ref, loss_ref,
):
    s0, s1, log_total = s0_ref[...], s1_ref[...], log_ref[...]
    count, half = s0.shape
    hot0, hot1 = hot(column_ref, s0.shape, 0), hot(column_ref, s0.shape, half)
    hi0, lo0 = split(jnp.exp(s0 - log_total) - hot0.astype(F32))
    mine_ref[...] = flip(hi0)
    both0_ref[:count], both0_ref[count:] = hi0, lo0
    hih, loh = split(jnp.exp(sh_ref[...] - log_total))
    hard_ref[...] = flip(hih, swapped(hih.shape[1], slots))
    bothh_ref[...] = jnp.concatenate([hih, loh], axis=1)
    hi1, lo1 = split(jnp.exp(s1 - log_total) - hot1.astype(F32))
    both1_ref[:count], both1_ref[count:] = hi1, lo1
    at_target = jnp.sum(jnp.where(hot0, s0, 0.0) + jnp.where(hot1, s1, 0.0), axis=1, keepdims=True)
    loss_ref[...] = log_total - at_target


def core_sum_kernel(first, coef_ref, q_ref, away_ref, *out_refs):
    n = out_refs[0].shape[0]
    coef = coef_ref[...]
    coef = coef[n : 3 * n] if first else jnp.concatenate([coef[:n], coef[3 * n :]], axis=0)

    def add(cols):
        total = dot(coef, q_ref[:, cols]) + away_ref[:, cols].astype(F32)
        for i, ref in enumerate(out_refs):
            ref[:, cols] = total[i * n : (i + 1) * n].astype(ref.dtype)

    over_columns(q_ref.shape[1], add)


def hard_grad_kernel(scale, coef_ref, q_ref, out_ref):
    places, slots, width = out_ref.shape

    def grad(cols):
        rows = scale * dot(coef_ref[...], q_ref[:, cols])
        for i in range(places):
            out_ref[i, :, cols] = rows[i * slots : (i + 1) * slots].astype(out_ref.dtype)

    over_columns(width, grad)


def query_grad_kernel(scale, c0, c1, ch, *refs):
    near, far, got = refs[:4], refs[4:8], refs[8]
    out, made, sems = refs[9:]
    count, width = made.shape
    copies = []

    def grad(cols):
        both = dot(c0[...], joined(near, cols)) + dot(c1[...], joined(far, cols))
        hard = got[:, cols]
        thin = dot(ch[...], jnp.concatenate([hard, hard], axis=0))
        made[:, cols] = (scale * (both[:count] + both[count:] + thin)).astype(made.dtype)
        copy = pltpu.make_async_copy(
            made.at[:, cols], out.at[0, :, cols], sems.at[len(copies)]
        )
        copy.start()
        copies.append(copy)

    over_columns(width, grad)
    for copy in copies:
        copy.wait()


def body(queries, passages, positives, hard_rows, hard_dest):
    q = queries[0]
    own = passages[0]
    targets = positives[0]
    owned_hard = hard_rows[0]
    count, width = q.shape
    rows = own.shape[0]
    groups = NY * NH
    slots = max(2, 2 * owned_hard.shape[0] // groups)
    half, places = NZ * NX * rows, groups * slots
    scale = width ** (-0.5)
    blk = lax.axis_index("blk")
    my_z, my_x, my_c = blk // (NX * NC), blk // NC % NX, blk % NC

    with jax.named_scope("gather_z"):
        z_rows = jnp.concatenate(exchange([own] * NZ, "blk", z_shift), axis=0)
    with jax.named_scope("hard_out"):
        packed, placing = call(
            functools.partial(pack_kernel, slots),
            [shape((places, width + FLAG)), shape((places, owned_hard.shape[0]))],
            (hard_dest.reshape(1, -1), owned_hard),
            "pack", 2 * places * owned_hard.size, 2,
        )
        from_y = swap(packed, Y_GROUPS)
        received = swap(turn(from_y, slots), H_GROUPS)
    with jax.named_scope("gather_x"):
        last, _ = lax.optimization_barrier((z_rows, from_y))
        near = exchange([z_rows] * (NX - 1) + [last], "blk", x_shift)
    with jax.named_scope("gather_core"):
        far = [lax.ppermute(x, "blk", CORE_SWAP) for x in near]

    owner = targets // rows
    o_z, o_x, o_c = owner // (NX * NC), owner // NC % NX, owner % NC
    column = (
        (o_c != my_c).astype(jnp.int32) * half
        + ((my_x - o_x) % NX * NZ + (my_z - o_z) % NZ) * rows
        + targets % rows
    )
    with jax.named_scope("scores"):
        [s0] = call(
            functools.partial(near_kernel, scale),
            [shape((count, half), F32)],
            (q, *near),
            "near", 2 * count * half * width, 8,
        )
        first, second, s1, sh, log_total = call(
            functools.partial(away_kernel, scale),
            [
                shape((half // 2, width)), shape((half // 2, width)), shape((count, half), F32),
                shape((count, places), F32), shape((count, 1), F32),
            ],
            (q, *far, received, s0, column.reshape(-1, 1)),
            "away", 4 * count * half * width, 10,
        )
        mine_rows, hard_cols, both0, both1, both_hard, loss_rows = call(
            functools.partial(coef_kernel, slots),
            [
                shape((half, count)), shape((places, count)), shape((2 * count, half)),
                shape((2 * count, half)), shape((count, 2 * places)), shape((count, 1), F32),
            ],
            (s0, s1, sh, log_total, column.reshape(-1, 1)),
            "coef", count * half * half, 8,
        )
    with jax.named_scope("scatter_core"):
        first = lax.ppermute(first, "blk", CORE_SWAP)
        second = lax.ppermute(second, "blk", CORE_SWAP)
    with jax.named_scope("scatter_x"):
        n = half // NX
        flops = count * half * width
        one, two = call(
            functools.partial(core_sum_kernel, True), [shape((n, width))] * 2,
            (mine_rows, q, first), "core_sum_first", flops, 8,
        )
        zero, three = call(
            functools.partial(core_sum_kernel, False), [shape((n, width), F32), shape((n, width))],
            (mine_rows, q, second), "core_sum_second", flops, 8,
        )
        chunks = [c.astype(F32) for c in exchange([zero, one, two, three], "blk", x_shift, -1)]
        mine_x = pieces(functools.reduce(jnp.add, chunks), NZ)

    hard_cols, _ = lax.optimization_barrier((hard_cols, second))
    with jax.named_scope("hard_back"):
        [g] = call(
            functools.partial(hard_grad_kernel, scale), [shape((groups, slots, width))],
            (hard_cols, q), "hard_grad", 2 * places * count * width, 4,
        )
        returned = lax.all_to_all(g, "group", split_axis=0, concat_axis=0, tiled=True)
        d_owned = t_dot(placing, returned.reshape(places, width)).astype(BF16)
    both0, _ = lax.optimization_barrier((both0, g))
    with jax.named_scope("d_query"):
        [d_query] = call(
            functools.partial(query_grad_kernel, scale),
            [shape((1, count, width))],
            (both0, both1, both_hard, *near, *far, received),
            "query_grad", 4 * count * (2 * half + places) * width, 12, pl.ANY,
            [pltpu.VMEM((count, width), BF16), pltpu.SemaphoreType.DMA((width // 1024,))],
        )
    with jax.named_scope("scatter_z"):
        sent = [mine_x[0]] + [m.astype(BF16) for m in mine_x[1:]]
        chunks = [c.astype(F32) for c in exchange(sent, "blk", z_shift, -1)]
        d_passage = (scale * functools.reduce(jnp.add, chunks)).astype(BF16)
    return (loss_rows.reshape(1, -1), d_query, d_passage[None], d_owned[None])


def solution(mesh):
    return jax.shard_map(
        body,
        mesh=mesh,
        in_specs=(
            P("group", "blk", None),
            P("group", "blk", None),
            P("group", "blk"),
            P("group", "blk", None),
            P("group", "blk", None),
        ),
        out_specs=(
            P("group", "blk"),
            P("group", "blk", None),
            P("group", "blk", None),
            P("group", "blk", None),
        ),
        check_vma=False,
    )
```

```python
import functools

import jax
import jax.numpy as jnp
from jax import lax
from jax.experimental import pallas as pl
from jax.experimental.pallas import tpu as pltpu
from jax.sharding import PartitionSpec as P

NZ, NX, NC = 4, 4, 2
NY, NH = 4, 4
Y_GROUPS = [[y * NH + h for y in range(NY)] for h in range(NH)]
H_GROUPS = [[y * NH + h for h in range(NH)] for y in range(NY)]
CORE_SWAP = [(i, i ^ 1) for i in range(NZ * NX * NC)]
FLAG = 128
BF16, F32 = jnp.bfloat16, jnp.float32


def z_shift(d):
    step = NX * NC
    return [(i, (i // step + d) % NZ * step + i % step) for i in range(NZ * step)]


def x_shift(d):
    step = NX * NC
    return [(i, i // step * step + (i + d * NC) % step) for i in range(NZ * step)]


def exchange(parts, axis, perm, sign=1):
    return parts[:1] + [lax.ppermute(p, axis, perm(sign * d)) for d, p in enumerate(parts) if d]


def pieces(x, n):
    k = x.shape[0] // n
    return [x[i * k : (i + 1) * k] for i in range(n)]


def dot_t(a, b):
    return lax.dot_general(a, b, (((1,), (1,)), ((), ())), preferred_element_type=F32)


def t_dot(a, b):
    return lax.dot_general(a, b, (((0,), (0,)), ((), ())), preferred_element_type=F32)


def dot(a, b):
    return jnp.dot(a, b, preferred_element_type=F32)


def split(a):
    hi = a.astype(BF16)
    return hi, (a - hi.astype(F32)).astype(BF16)


def swap(x, members):
    return lax.all_to_all(
        x, "group", split_axis=0, concat_axis=0, axis_index_groups=members, tiled=True
    )


def iota(dims, dim):
    return lax.broadcasted_iota(jnp.int32, dims, dim)


def shape(dims, dtype=BF16):
    return jax.ShapeDtypeStruct(dims, dtype)


def call(kernel, outs, args, name, flops, grant, hbm=0, scratch=()):
    size = sum(a.size * a.dtype.itemsize for a in (*args, *outs))
    return pl.pallas_call(
        kernel,
        in_specs=[pl.BlockSpec(memory_space=pltpu.VMEM)] * len(args),
        out_specs=[pl.BlockSpec(memory_space=pltpu.VMEM)] * (len(outs) - hbm)
        + [pl.BlockSpec(memory_space=pltpu.HBM)] * hbm,
        out_shape=outs,
        scratch_shapes=scratch,
        cost_estimate=pl.CostEstimate(flops=flops, bytes_accessed=size, transcendentals=0),
        compiler_params=pltpu.CompilerParams(vmem_limit_bytes=grant << 20),
        name=name,
    )(*args)


def over_columns(width, step, block=1024):
    for i in range(0, width, block):
        step(slice(i, i + block))


def joined(refs, cols=slice(None)):
    return jnp.concatenate([r[:, cols] for r in refs], axis=0)


def flip(x, pick=None):
    n = x.shape[1]
    pick = iota((n, n), 0) == iota((n, n), 1) if pick is None else pick
    return dot_t(pick.astype(BF16), x).astype(BF16)


def swapped(n, slots):
    row, col = iota((n, n), 0), iota((n, n), 1)
    place = row // slots
    return (place % NH * NY + place // NH) * slots + row % slots == col


def turn_kernel(slots, in_ref, out_ref):
    pick = swapped(in_ref.shape[0], slots).astype(BF16)
    out_ref[...] = dot(pick, in_ref[...]).astype(BF16)


def turn(x, slots):
    [out] = call(
        functools.partial(turn_kernel, slots), [shape(x.shape)], (x,),
        "turn", 2 * x.shape[0] * x.size, 2,
    )
    return out


def pack_kernel(slots, dest_ref, rows_ref, packed_ref, placing_ref):
    dest = dest_ref[...]
    count, width = rows_ref.shape
    groups = NY * NH
    hot = (dest == iota((groups, count), 0)).astype(F32)
    ahead = (iota((count, count), 0) < iota((count, count), 1)).astype(F32)
    rank = jnp.sum(dot(hot, ahead) * hot, axis=0, keepdims=True).astype(jnp.int32)
    at = iota((groups * slots, count), 0)
    send = (dest * slots + rank == at).astype(BF16)
    packed_ref[:, :width] = dot(send, rows_ref[...]).astype(BF16)
    packed_ref[:, width:] = dot(send, jnp.ones((count, FLAG), BF16)).astype(BF16)
    placing_ref[...] = send


def near_kernel(scale, q_ref, *refs):
    refs[-1][...] = scale * dot_t(q_ref[...], joined(refs[:-1]))


def hot(column_ref, dims, start):
    return column_ref[...] == iota(dims, 1) + start


def away_kernel(
    scale, q_ref, far0, far1, far2, far3, got_ref, s0_ref, column_ref,
    first_ref, second_ref, s1_ref, sh_ref, log_ref,
):
    count, width = q_ref.shape
    q, s0 = q_ref[...], s0_ref[...]
    half = s0.shape[1]
    flags = dot_t(jnp.ones((count, FLAG), BF16), got_ref[:, width:])
    sh = jnp.where(flags > 0.5 * FLAG, scale * dot_t(q, got_ref[:, :width]), -jnp.inf)
    s1 = scale * dot_t(q, joined((far0, far1, far2, far3)))
    top = jnp.maximum(
        jnp.max(jnp.maximum(s0, s1), axis=1, keepdims=True), jnp.max(sh, axis=1, keepdims=True)
    )
    total = jnp.sum(jnp.exp(s0 - top) + jnp.exp(s1 - top), axis=1, keepdims=True)
    total = total + jnp.sum(jnp.exp(sh - top), axis=1, keepdims=True)
    log_total = top + jnp.log(total)
    c1 = jnp.exp(s1 - log_total) - hot(column_ref, (count, half), half).astype(F32)
    away = flip(c1.astype(BF16))
    n = half // NX

    def send(cols):
        rows = dot(away, q_ref[:, cols]).astype(BF16)
        first_ref[:, cols] = rows[n : 3 * n]
        second_ref[:n, cols], second_ref[n:, cols] = rows[:n], rows[3 * n :]

    over_columns(width, send)
    s1_ref[...], sh_ref[...], log_ref[...] = s1, sh, log_total


def mine_kernel(s_ref, log_ref, column_ref, out_ref):
    coef = jnp.exp(s_ref[...] - log_ref[...]) - hot(column_ref, s_ref.shape, 0).astype(F32)
    out_ref[...] = flip(coef.astype(BF16))


def core_sum_kernel(start, skip, coef_ref, q_ref, away_ref, *out_refs):
    n = out_refs[0].shape[0]
    rows = n * len(out_refs)

    def add(cols):
        total = dot(coef_ref[start : start + rows], q_ref[:, cols])
        total = total + away_ref[skip : skip + rows, cols].astype(F32)
        for i, ref in enumerate(out_refs):
            ref[:, cols] = total[i * n : (i + 1) * n].astype(ref.dtype)

    over_columns(q_ref.shape[1], add)


def rest_kernel(
    scale, slots, s0_ref, s1_ref, sh_ref, log_ref, column_ref, mine_ref, q_ref, away_ref,
    hard_ref, bothh_ref, loss_ref, both0_ref, both1_ref, own_ref,
    made0, made1, made_own, sems,
):
    s0, s1, log_total = s0_ref[...], s1_ref[...], log_ref[...]
    count, half = s0.shape
    copies = [
        pltpu.make_async_copy(made, out, sems.at[i])
        for i, (made, out) in enumerate(
            ((made_own, own_ref), (made0, both0_ref), (made1, both1_ref))
        )
    ]
    core_sum_kernel(0, 0, mine_ref, q_ref, away_ref, made_own)
    copies[0].start()
    hot0, hot1 = hot(column_ref, s0.shape, 0), hot(column_ref, s0.shape, half)
    made0[:count], made0[count:] = split(jnp.exp(s0 - log_total) - hot0.astype(F32))
    copies[1].start()
    made1[:count], made1[count:] = split(jnp.exp(s1 - log_total) - hot1.astype(F32))
    copies[2].start()
    hih, loh = split(jnp.exp(sh_ref[...] - log_total))
    bothh_ref[...] = jnp.concatenate([hih, loh], axis=1)
    coef = flip(hih, swapped(hih.shape[1], slots))

    def grad(cols):
        rows = scale * dot(coef, q_ref[:, cols])
        for i in range(hard_ref.shape[0]):
            hard_ref[i, :, cols] = rows[i * slots : (i + 1) * slots].astype(BF16)

    over_columns(q_ref.shape[1], grad)
    at_target = jnp.sum(jnp.where(hot0, s0, 0.0) + jnp.where(hot1, s1, 0.0), axis=1, keepdims=True)
    loss_ref[...] = log_total - at_target
    for copy in copies:
        copy.wait()


def query_grad_kernel(scale, c0, c1, ch, *refs):
    near, far, got = refs[:4], refs[4:8], refs[8]
    out, made, sems = refs[9:]
    count, width = made.shape
    copies = []

    def grad(cols):
        both = dot(c0[...], joined(near, cols)) + dot(c1[...], joined(far, cols))
        hard = got[:, cols]
        thin = dot(ch[...], jnp.concatenate([hard, hard], axis=0))
        made[:, cols] = (scale * (both[:count] + both[count:] + thin)).astype(made.dtype)
        copy = pltpu.make_async_copy(
            made.at[:, cols], out.at[0, :, cols], sems.at[len(copies)]
        )
        copy.start()
        copies.append(copy)

    over_columns(width, grad)
    for copy in copies:
        copy.wait()


def body(queries, passages, positives, hard_rows, hard_dest):
    q = queries[0]
    own = passages[0]
    targets = positives[0]
    owned_hard = hard_rows[0]
    count, width = q.shape
    rows = own.shape[0]
    groups = NY * NH
    slots = max(2, 2 * owned_hard.shape[0] // groups)
    half, places = NZ * NX * rows, groups * slots
    scale = width ** (-0.5)
    blk = lax.axis_index("blk")
    my_z, my_x, my_c = blk // (NX * NC), blk // NC % NX, blk % NC

    with jax.named_scope("gather_z"):
        z_rows = jnp.concatenate(exchange([own] * NZ, "blk", z_shift), axis=0)
    with jax.named_scope("hard_out"):
        packed, placing = call(
            functools.partial(pack_kernel, slots),
            [shape((places, width + FLAG)), shape((places, owned_hard.shape[0]))],
            (hard_dest.reshape(1, -1), owned_hard),
            "pack", 2 * places * owned_hard.size, 2,
        )
        from_y = swap(packed, Y_GROUPS)
        received = swap(turn(from_y, slots), H_GROUPS)
    with jax.named_scope("gather_x"):
        last, _ = lax.optimization_barrier((z_rows, from_y))
        near = exchange([z_rows] * (NX - 1) + [last], "blk", x_shift)
    with jax.named_scope("gather_core"):
        far = [lax.ppermute(x, "blk", CORE_SWAP) for x in near]

    owner = targets // rows
    o_z, o_x, o_c = owner // (NX * NC), owner // NC % NX, owner % NC
    column = (
        (o_c != my_c).astype(jnp.int32) * half
        + ((my_x - o_x) % NX * NZ + (my_z - o_z) % NZ) * rows
        + targets % rows
    )
    with jax.named_scope("scores"):
        [s0] = call(
            functools.partial(near_kernel, scale),
            [shape((count, half), F32)],
            (q, *near),
            "near", 2 * count * half * width, 8,
        )
        first, second, s1, sh, log_total = call(
            functools.partial(away_kernel, scale),
            [
                shape((half // 2, width)), shape((half // 2, width)), shape((count, half), F32),
                shape((count, places), F32), shape((count, 1), F32),
            ],
            (q, *far, received, s0, column.reshape(-1, 1)),
            "away", 4 * count * half * width, 10,
        )
        [mine_rows] = call(
            mine_kernel, [shape((half, count))], (s0, log_total, column.reshape(-1, 1)),
            "mine", 2 * count * half * half, 4,
        )
    with jax.named_scope("scatter_core"):
        first = lax.ppermute(first, "blk", CORE_SWAP)
        second = lax.ppermute(second, "blk", CORE_SWAP)
    with jax.named_scope("scatter_x"):
        n = half // NX
        flops = count * half * width
        [three] = call(
            functools.partial(core_sum_kernel, 3 * n, n), [shape((n, width))],
            (mine_rows, q, second), "core_sum_second", flops // 2, 8,
        )
        one, two = call(
            functools.partial(core_sum_kernel, n, 0), [shape((n, width))] * 2,
            (mine_rows, q, first), "core_sum_first", flops, 8,
        )
    with jax.named_scope("rest"):
        parts = shape((2 * count, half))
        g, both_hard, loss_rows, both0, both1, zero = call(
            functools.partial(rest_kernel, scale, slots),
            [
                shape((groups, slots, width)), shape((count, 2 * places)), shape((count, 1), F32),
                parts, parts, shape((n, width), F32),
            ],
            (s0, s1, sh, log_total, column.reshape(-1, 1), mine_rows, q, second),
            "rest", flops, 12, 3,
            [
                pltpu.VMEM(parts.shape, BF16), pltpu.VMEM(parts.shape, BF16),
                pltpu.VMEM((n, width), F32), pltpu.SemaphoreType.DMA((3,)),
            ],
        )
    with jax.named_scope("scatter_x"):
        chunks = [c.astype(F32) for c in exchange([zero, one, two, three], "blk", x_shift, -1)]
        mine_x = pieces(functools.reduce(jnp.add, chunks), NZ)
    with jax.named_scope("hard_back"):
        returned = lax.all_to_all(g, "group", split_axis=0, concat_axis=0, tiled=True)
        d_owned = t_dot(placing, returned.reshape(places, width)).astype(BF16)
    with jax.named_scope("d_query"):
        [d_query] = call(
            functools.partial(query_grad_kernel, scale),
            [shape((1, count, width))],
            (both0, both1, both_hard, *near, *far, received),
            "query_grad", 4 * count * (2 * half + places) * width, 12, 1,
            [pltpu.VMEM((count, width), BF16), pltpu.SemaphoreType.DMA((width // 1024,))],
        )
    with jax.named_scope("scatter_z"):
        sent = [mine_x[0]] + [m.astype(BF16) for m in mine_x[1:]]
        chunks = [c.astype(F32) for c in exchange(sent, "blk", z_shift, -1)]
        d_passage = (scale * functools.reduce(jnp.add, chunks)).astype(BF16)
    return (loss_rows.reshape(1, -1), d_query, d_passage[None], d_owned[None])


def solution(mesh):
    return jax.shard_map(
        body,
        mesh=mesh,
        in_specs=(
            P("group", "blk", None),
            P("group", "blk", None),
            P("group", "blk"),
            P("group", "blk", None),
            P("group", "blk", None),
        ),
        out_specs=(
            P("group", "blk"),
            P("group", "blk", None),
            P("group", "blk", None),
            P("group", "blk", None),
        ),
        check_vma=False,
    )
```

```python
import functools

import jax
import jax.numpy as jnp
from jax import lax
from jax.experimental import pallas as pl
from jax.experimental.pallas import tpu as pltpu
from jax.sharding import PartitionSpec as P

NZ, NX, NC = 4, 4, 2
NY, NH = 4, 4
Y_GROUPS = [[y * NH + h for y in range(NY)] for h in range(NH)]
H_GROUPS = [[y * NH + h for h in range(NH)] for y in range(NY)]
CORE_SWAP = [(i, i ^ 1) for i in range(NZ * NX * NC)]
FLAG = 128
BF16, F32 = jnp.bfloat16, jnp.float32


def z_shift(d):
    step = NX * NC
    return [(i, (i // step + d) % NZ * step + i % step) for i in range(NZ * step)]


def x_shift(d):
    step = NX * NC
    return [(i, i // step * step + (i + d * NC) % step) for i in range(NZ * step)]


def exchange(parts, axis, perm, sign=1):
    return parts[:1] + [lax.ppermute(p, axis, perm(sign * d)) for d, p in enumerate(parts) if d]


def pieces(x, n):
    k = x.shape[0] // n
    return [x[i * k : (i + 1) * k] for i in range(n)]


def dot_t(a, b):
    return lax.dot_general(a, b, (((1,), (1,)), ((), ())), preferred_element_type=F32)


def t_dot(a, b):
    return lax.dot_general(a, b, (((0,), (0,)), ((), ())), preferred_element_type=F32)


def dot(a, b):
    return jnp.dot(a, b, preferred_element_type=F32)


def split(a):
    hi = a.astype(BF16)
    return hi, (a - hi.astype(F32)).astype(BF16)


def swap(x, members):
    return lax.all_to_all(
        x, "group", split_axis=0, concat_axis=0, axis_index_groups=members, tiled=True
    )


def iota(dims, dim):
    return lax.broadcasted_iota(jnp.int32, dims, dim)


def shape(dims, dtype=BF16):
    return jax.ShapeDtypeStruct(dims, dtype)


def call(kernel, outs, args, name, flops, grant, hbm=0, scratch=()):
    size = sum(a.size * a.dtype.itemsize for a in (*args, *outs))
    return pl.pallas_call(
        kernel,
        in_specs=[pl.BlockSpec(memory_space=pltpu.VMEM)] * len(args),
        out_specs=[pl.BlockSpec(memory_space=pltpu.VMEM)] * (len(outs) - hbm)
        + [pl.BlockSpec(memory_space=pltpu.HBM)] * hbm,
        out_shape=outs,
        scratch_shapes=scratch,
        cost_estimate=pl.CostEstimate(flops=flops, bytes_accessed=size, transcendentals=0),
        compiler_params=pltpu.CompilerParams(vmem_limit_bytes=grant << 20),
        name=name,
    )(*args)


def over_columns(width, step, block=1024):
    for i in range(0, width, block):
        step(slice(i, i + block))


def joined(refs, cols=slice(None)):
    return jnp.concatenate([r[:, cols] for r in refs], axis=0)


def flip(x, pick=None):
    n = x.shape[1]
    pick = iota((n, n), 0) == iota((n, n), 1) if pick is None else pick
    return dot_t(pick.astype(BF16), x).astype(BF16)


def swapped(n, slots):
    row, col = iota((n, n), 0), iota((n, n), 1)
    place = row // slots
    return (place % NH * NY + place // NH) * slots + row % slots == col


def turn_kernel(slots, in_ref, out_ref):
    pick = swapped(in_ref.shape[0], slots).astype(BF16)
    out_ref[...] = dot(pick, in_ref[...]).astype(BF16)


def turn(x, slots):
    [out] = call(
        functools.partial(turn_kernel, slots), [shape(x.shape)], (x,),
        "turn", 2 * x.shape[0] * x.size, 2,
    )
    return out


def pack_kernel(slots, dest_ref, rows_ref, packed_ref, placing_ref):
    dest = dest_ref[...]
    count, width = rows_ref.shape
    groups = NY * NH
    hot = (dest == iota((groups, count), 0)).astype(F32)
    ahead = (iota((count, count), 0) < iota((count, count), 1)).astype(F32)
    rank = jnp.sum(dot(hot, ahead) * hot, axis=0, keepdims=True).astype(jnp.int32)
    at = iota((groups * slots, count), 0)
    send = (dest * slots + rank == at).astype(BF16)
    packed_ref[:, :width] = dot(send, rows_ref[...]).astype(BF16)
    packed_ref[:, width:] = dot(send, jnp.ones((count, FLAG), BF16)).astype(BF16)
    placing_ref[...] = send


def near_kernel(scale, q_ref, *refs):
    refs[-1][...] = scale * dot_t(q_ref[...], joined(refs[:-1]))


def hot(column_ref, dims, start):
    return column_ref[...] == iota(dims, 1) + start


def away_kernel(
    scale, q_ref, far0, far1, far2, far3, got_ref, s0_ref, column_ref,
    first_ref, second_ref, s1_ref, sh_ref, log_ref,
):
    count, width = q_ref.shape
    q, s0 = q_ref[...], s0_ref[...]
    half = s0.shape[1]
    flags = dot_t(jnp.ones((count, FLAG), BF16), got_ref[:, width:])
    sh = jnp.where(flags > 0.5 * FLAG, scale * dot_t(q, got_ref[:, :width]), -jnp.inf)
    s1 = scale * dot_t(q, joined((far0, far1, far2, far3)))
    top = jnp.maximum(
        jnp.max(jnp.maximum(s0, s1), axis=1, keepdims=True), jnp.max(sh, axis=1, keepdims=True)
    )
    total = jnp.sum(jnp.exp(s0 - top) + jnp.exp(s1 - top), axis=1, keepdims=True)
    total = total + jnp.sum(jnp.exp(sh - top), axis=1, keepdims=True)
    log_total = top + jnp.log(total)
    c1 = jnp.exp(s1 - log_total) - hot(column_ref, (count, half), half).astype(F32)
    away = flip(c1.astype(BF16))
    n = half // NX

    def send(cols):
        rows = dot(away, q_ref[:, cols]).astype(BF16)
        first_ref[:, cols] = rows[n : 3 * n]
        second_ref[:n, cols], second_ref[n:, cols] = rows[:n], rows[3 * n :]

    over_columns(width, send)
    s1_ref[...], sh_ref[...], log_ref[...] = s1, sh, log_total


def mine_kernel(s_ref, log_ref, column_ref, out_ref):
    coef = jnp.exp(s_ref[...] - log_ref[...]) - hot(column_ref, s_ref.shape, 0).astype(F32)
    out_ref[...] = flip(coef.astype(BF16))


def core_sum_kernel(start, skip, coef_ref, q_ref, away_ref, *out_refs):
    n = out_refs[0].shape[0]
    rows = n * len(out_refs)

    def add(cols):
        total = dot(coef_ref[start : start + rows], q_ref[:, cols])
        total = total + away_ref[skip : skip + rows, cols].astype(F32)
        for i, ref in enumerate(out_refs):
            ref[:, cols] = total[i * n : (i + 1) * n].astype(ref.dtype)

    over_columns(q_ref.shape[1], add)


def rest_kernel(
    scale, slots, s0_ref, s1_ref, sh_ref, log_ref, column_ref, mine_ref, q_ref, away_ref,
    hard_ref, bothh_ref, loss_ref, both0_ref, both1_ref, own_ref,
    made0, made1, made_own, sems,
):
    s0, s1, log_total = s0_ref[...], s1_ref[...], log_ref[...]
    count, half = s0.shape
    copies = [
        pltpu.make_async_copy(made, out, sems.at[i])
        for i, (made, out) in enumerate(
            ((made_own, own_ref), (made0, both0_ref), (made1, both1_ref))
        )
    ]
    core_sum_kernel(0, 0, mine_ref, q_ref, away_ref, made_own)
    copies[0].start()
    hot0, hot1 = hot(column_ref, s0.shape, 0), hot(column_ref, s0.shape, half)
    made0[:count], made0[count:] = split(jnp.exp(s0 - log_total) - hot0.astype(F32))
    copies[1].start()
    made1[:count], made1[count:] = split(jnp.exp(s1 - log_total) - hot1.astype(F32))
    copies[2].start()
    hih, loh = split(jnp.exp(sh_ref[...] - log_total))
    bothh_ref[...] = jnp.concatenate([hih, loh], axis=1)
    coef = flip(hih, swapped(hih.shape[1], slots))

    def grad(cols):
        rows = scale * dot(coef, q_ref[:, cols])
        for i in range(hard_ref.shape[0]):
            hard_ref[i, :, cols] = rows[i * slots : (i + 1) * slots].astype(BF16)

    over_columns(q_ref.shape[1], grad)
    at_target = jnp.sum(jnp.where(hot0, s0, 0.0) + jnp.where(hot1, s1, 0.0), axis=1, keepdims=True)
    loss_ref[...] = log_total - at_target
    for copy in copies:
        copy.wait()


def x_sum_kernel(*refs):
    chunks, outs, held, sems = refs[:NX], refs[NX : NX + NZ], refs[NX + NZ : -1], refs[-1]
    copies = [
        pltpu.make_async_copy(c, h, sems.at[i]) for i, (c, h) in enumerate(zip(chunks, held))
    ]
    for copy in copies:
        copy.start()
    for copy in copies:
        copy.wait()
    total = functools.reduce(jnp.add, [h[...].astype(F32) for h in held])
    n = outs[0].shape[0]
    for d, ref in enumerate(outs):
        ref[...] = total[d * n : (d + 1) * n].astype(ref.dtype)


def query_grad_kernel(scale, c0, c1, ch, *refs):
    near, far, got = refs[:4], refs[4:8], refs[8]
    out, made, sems = refs[9:]
    count, width = made.shape
    copies = []

    def grad(cols):
        both = dot(c0[...], joined(near, cols)) + dot(c1[...], joined(far, cols))
        hard = got[:, cols]
        thin = dot(ch[...], jnp.concatenate([hard, hard], axis=0))
        made[:, cols] = (scale * (both[:count] + both[count:] + thin)).astype(made.dtype)
        copy = pltpu.make_async_copy(
            made.at[:, cols], out.at[0, :, cols], sems.at[len(copies)]
        )
        copy.start()
        copies.append(copy)

    over_columns(width, grad)
    for copy in copies:
        copy.wait()


def body(queries, passages, positives, hard_rows, hard_dest):
    q = queries[0]
    own = passages[0]
    targets = positives[0]
    owned_hard = hard_rows[0]
    count, width = q.shape
    rows = own.shape[0]
    groups = NY * NH
    slots = max(2, 2 * owned_hard.shape[0] // groups)
    half, places = NZ * NX * rows, groups * slots
    scale = width ** (-0.5)
    blk = lax.axis_index("blk")
    my_z, my_x, my_c = blk // (NX * NC), blk // NC % NX, blk % NC

    with jax.named_scope("gather_z"):
        z_rows = jnp.concatenate(exchange([own] * NZ, "blk", z_shift), axis=0)
    with jax.named_scope("hard_out"):
        packed, placing = call(
            functools.partial(pack_kernel, slots),
            [shape((places, width + FLAG)), shape((places, owned_hard.shape[0]))],
            (hard_dest.reshape(1, -1), owned_hard),
            "pack", 2 * places * owned_hard.size, 2,
        )
        from_y = swap(packed, Y_GROUPS)
        received = swap(turn(from_y, slots), H_GROUPS)
    with jax.named_scope("gather_x"):
        last, _ = lax.optimization_barrier((z_rows, from_y))
        near = exchange([z_rows] * (NX - 1) + [last], "blk", x_shift)
    with jax.named_scope("gather_core"):
        far = [lax.ppermute(x, "blk", CORE_SWAP) for x in near]

    owner = targets // rows
    o_z, o_x, o_c = owner // (NX * NC), owner // NC % NX, owner % NC
    column = (
        (o_c != my_c).astype(jnp.int32) * half
        + ((my_x - o_x) % NX * NZ + (my_z - o_z) % NZ) * rows
        + targets % rows
    )
    with jax.named_scope("scores"):
        [s0] = call(
            functools.partial(near_kernel, scale),
            [shape((count, half), F32)],
            (q, *near),
            "near", 2 * count * half * width, 8,
        )
        first, second, s1, sh, log_total = call(
            functools.partial(away_kernel, scale),
            [
                shape((half // 2, width)), shape((half // 2, width)), shape((count, half), F32),
                shape((count, places), F32), shape((count, 1), F32),
            ],
            (q, *far, received, s0, column.reshape(-1, 1)),
            "away", 4 * count * half * width, 10,
        )
        [mine_rows] = call(
            mine_kernel, [shape((half, count))], (s0, log_total, column.reshape(-1, 1)),
            "mine", 2 * count * half * half, 4,
        )
    with jax.named_scope("scatter_core"):
        first = lax.ppermute(first, "blk", CORE_SWAP)
        second = lax.ppermute(second, "blk", CORE_SWAP)
    with jax.named_scope("scatter_x"):
        n = half // NX
        flops = count * half * width
        [three] = call(
            functools.partial(core_sum_kernel, 3 * n, n), [shape((n, width))],
            (mine_rows, q, second), "core_sum_second", flops // 2, 8,
        )
        one, two = call(
            functools.partial(core_sum_kernel, n, 0), [shape((n, width))] * 2,
            (mine_rows, q, first), "core_sum_first", flops, 8,
        )
    with jax.named_scope("rest"):
        parts = shape((2 * count, half))
        g, both_hard, loss_rows, both0, both1, zero = call(
            functools.partial(rest_kernel, scale, slots),
            [
                shape((groups, slots, width)), shape((count, 2 * places)), shape((count, 1), F32),
                parts, parts, shape((n, width), F32),
            ],
            (s0, s1, sh, log_total, column.reshape(-1, 1), mine_rows, q, second),
            "rest", flops, 12, 3,
            [
                pltpu.VMEM(parts.shape, BF16), pltpu.VMEM(parts.shape, BF16),
                pltpu.VMEM((n, width), F32), pltpu.SemaphoreType.DMA((3,)),
            ],
        )
    with jax.named_scope("scatter_x"):
        chunks = exchange([zero, one, two, three], "blk", x_shift, -1)
        loss_rows = loss_rows.reshape(1, -1)
        chunks[1], loss_rows = lax.optimization_barrier((chunks[1], loss_rows))
        mine_x = pl.pallas_call(
            x_sum_kernel,
            in_specs=[pl.BlockSpec(memory_space=pltpu.HBM)] * NX,
            out_specs=[pl.BlockSpec(memory_space=pltpu.VMEM)] * NZ,
            out_shape=[shape((rows, width), F32)] + [shape((rows, width))] * (NZ - 1),
            scratch_shapes=[pltpu.VMEM(c.shape, c.dtype) for c in chunks]
            + [pltpu.SemaphoreType.DMA((NX,))],
            cost_estimate=pl.CostEstimate(
                flops=4 * n * width, bytes_accessed=12 * n * width, transcendentals=0
            ),
            compiler_params=pltpu.CompilerParams(vmem_limit_bytes=8 << 20),
            name="x_sum",
        )(*chunks)
    with jax.named_scope("hard_back"):
        returned = lax.all_to_all(g, "group", split_axis=0, concat_axis=0, tiled=True)
        d_owned = t_dot(placing, returned.reshape(places, width)).astype(BF16)
    with jax.named_scope("d_query"):
        [d_query] = call(
            functools.partial(query_grad_kernel, scale),
            [shape((1, count, width))],
            (both0, both1, both_hard, *near, *far, received),
            "query_grad", 4 * count * (2 * half + places) * width, 12, 1,
            [pltpu.VMEM((count, width), BF16), pltpu.SemaphoreType.DMA((width // 1024,))],
        )
    with jax.named_scope("scatter_z"):
        chunks = [c.astype(F32) for c in exchange(list(mine_x), "blk", z_shift, -1)]
        d_passage = (scale * functools.reduce(jnp.add, chunks)).astype(BF16)
    return (loss_rows, d_query, d_passage[None], d_owned[None])


def solution(mesh):
    return jax.shard_map(
        body,
        mesh=mesh,
        in_specs=(
            P("group", "blk", None),
            P("group", "blk", None),
            P("group", "blk"),
            P("group", "blk", None),
            P("group", "blk", None),
        ),
        out_specs=(
            P("group", "blk"),
            P("group", "blk", None),
            P("group", "blk", None),
            P("group", "blk", None),
        ),
        check_vma=False,
    )
```
